32 devices in a mesh: groups: 2 (over y), attn: 4 (over x, core), exp: 4 (over z).
Axes of the slice: x: 2, y: 2, z: 4, core: 2. Of those that a mesh axis runs over, the one named last changes fastest.
Arguments:
- queries: bfloat16 [64, 32, 4096], P(('groups', 'exp'), None, 'attn'), parts along dimension 0, may hold values from -20 to 20
- new_keys: bfloat16 [64, 32, 512], P(('groups', 'exp'), None, 'attn'), parts along dimension 0, may hold values from -4 to 4
- new_values: bfloat16 [64, 32, 512], P(('groups', 'exp'), None, 'attn'), parts along dimension 0, may hold values from -4 to 4
- cache_keys: bfloat16 [64, 256, 512], P(('groups', 'exp'), None, 'attn'), parts along dimension 0, may hold values from -4 to 4
- cache_values: bfloat16 [64, 256, 512], P(('groups', 'exp'), None, 'attn'), parts along dimension 0, may hold values from -4 to 4
- cache_len: int32 [64], P(('groups', 'exp')), parts along dimension 0, may hold values from 2 to 256, as said below
- out_weight: bfloat16 [4096, 2048], P('attn', 'exp'), may hold values from -4 to 4
- residual: float32 [2048, 2048], P(('groups', 'exp', 'attn')), parts along dimension 0, may hold values from -6 to 6
- norm_gain: float32 [2048], replicated, may hold values from 0.1 to 1.9
- expert_ids: int32 [2048, 8], P(('groups', 'exp', 'attn')), parts along dimension 0, may hold values from 0 to 15, all different within a row; in each aligned block of 64 rows (0 to 63, 64 to 127, ...) at most 64 rows name the same one
- gate_nums: int32 [2048, 8], P(('groups', 'exp', 'attn')), parts along dimension 0, may hold values from 1 to 16
- w_gate_up: bfloat16 [16, 2048, 1536], P(('attn', 'exp')), may hold values from -0.125 to 0.125
- w_down: bfloat16 [16, 768, 2048], P(('attn', 'exp')), may hold values from -0.21875 to 0.21875
Outputs:
- mixed: float32 [2048, 2048], P(('groups', 'exp', 'attn')), parts along dimension 0
The draws below stay inside these ranges and needn't reach their ends.
There are 2 independent parts, one for each index of `groups`. The reference program is written for one: setup_inputs(seed, part) draws one part's arguments, and reference() takes and returns one part's arrays. A program takes and returns all parts, laid end to end along the dimension named above; an argument that names none is the same for every part. Nothing has to cross between parts.
Inputs may be any that keep to these rules, and one draw needn't show every extreme that they name: `cache_len`: number of valid cache slots of each session; some session has all 256. `expert_ids`: within the 64 rows of one device, no expert is named by more than 64 rows, and this bound is reached; each row names 8 distinct experts.
All inputs are finite; a program needn't handle non-finite values.
Results may differ from the reference program's by a relative error of at most 0.0038.
Values may be sent and summed in bfloat16 or wider, within the bound.
A program may use at most 128 MiB of HBM per device.

```python
import math
import jax
import jax.numpy as jnp
import numpy as np
from jax import lax

D = 2048
HEADS = 32
KVH = 4
HD = 128
MOE_FF = 768
TOP = 8
CACHE = 256
NEW = 32
SESSIONS = 32
TOKENS = 1024
TOK_DEV = 64
EXPERTS = 16
CAP = 64
N_ATTN = 4
N_EXP = 4


def shared_keys(key):
    keys = jnp.clip(jax.random.normal(jax.random.fold_in(key, 11), (SESSIONS, CACHE, KVH * HD), jnp.float32), -4.0, 4.0)
    return keys


def draw_cache_keys(key, part):
    keys = shared_keys(key)
    return keys.astype(jnp.bfloat16)


def draw_queries(key, part):
    base = jnp.clip(jax.random.normal(jax.random.fold_in(key, 21), (SESSIONS, NEW, HEADS * HD), jnp.float32), -4.0, 4.0)
    return base.astype(jnp.bfloat16)


def draw_cache_len(key, part):
    lengths = jax.random.randint(jax.random.fold_in(key, 31), (SESSIONS,), 2, CACHE + 1)
    where_full = jax.random.randint(jax.random.fold_in(key, 32), (), 0, SESSIONS)
    return jnp.where(jnp.arange(SESSIONS) == where_full, CACHE, lengths).astype(jnp.int32)


def touch_ends(drawn, rng, low, high):
    place = [jax.random.randint(jax.random.fold_in(rng, axis), (), 0, length) for axis, length in enumerate(drawn.shape)]
    longest = drawn.shape.index(max(drawn.shape))
    next_to = place[:longest] + [(place[longest] + 1) % drawn.shape[longest]] + place[longest + 1:]
    return drawn.at[tuple(place)].set(low).at[tuple(next_to)].set(high)


def shard_levels(stream_key, shape, pieces, least, top_value):
    level = 1.0
    for axis_at, parts in pieces:
        heights = jax.random.uniform(jax.random.fold_in(jax.random.fold_in(stream_key, 6), axis_at), (parts,), jnp.float32, least / len(pieces), top_value / len(pieces))
        level = level * jnp.repeat(jnp.exp(heights), shape[axis_at] // parts).reshape((-1,) + (1,) * (len(shape) - 1 - axis_at))
    return level


def routed_block(own_key, own, number, rows, number_of, top, reach, skew):
    ranking = jax.random.permutation(own_key, number_of)
    crowded, common = load_shares(number_of, rows * top, reach, skew, True), load_shares(number_of, rows * top, reach, skew, False)
    places = jnp.arange(number_of)

    def named(tallies, rotation):
        used = int((tallies > 0).sum())
        fixed = max(1, used // 4)
        shifted = fixed + (places - fixed + rotation * (used - fixed)) % max(1, number_of - fixed)
        return jnp.zeros((number_of,), jnp.int32).at[ranking[jnp.where(places < fixed, places, shifted)]].set(jnp.asarray(tallies, jnp.int32))

    tallies = jnp.where(number % 4 == 0, named(crowded, number // 4), named(common, number - number // 4 - 1))
    mixed = jax.random.permutation(jax.random.fold_in(own, 3), number_of)
    donor, taker = mixed[0:number_of // 2 * 2:2], mixed[1:number_of // 2 * 2:2]
    margin = jnp.minimum(tallies[donor] - 1, reach - tallies[taker]) // 2
    margin = jnp.where((donor == ranking[0]) | (taker == ranking[0]) | (tallies[taker] == 0), 0, jnp.maximum(margin, 0))
    shifted = jax.random.randint(jax.random.fold_in(own, 4), (number_of // 2,), 0, 1 << 20) % (margin + 1)
    tallies = tallies.at[donor].add(-shifted).at[taker].add(shifted)
    items = jnp.searchsorted(jnp.cumsum(tallies), jnp.arange(rows * top), side="right").astype(jnp.int32)
    table = items.reshape(top, rows).T
    table = table[jax.random.permutation(jax.random.fold_in(own, 1), rows)]
    rotation = jax.random.randint(jax.random.fold_in(own, 2), (rows, 1), 0, top)
    return jnp.take_along_axis(table, (jnp.arange(top)[None, :] + rotation) % top, axis=1)


def load_shares(amount, total, reach, slope, full):
    weights = [(1 << 20) // math.isqrt(rank ** slope) + 1 for rank in range(1, amount + 1)]
    largest = reach if full else min(reach, max(-(-total // amount), total * weights[0] // sum(weights)))
    least = 1 if total - largest >= amount - 1 else 0
    holding, surplus = [largest] + [least] * (amount - 1), total - largest - least * (amount - 1)
    while surplus > 0:
        free = [i for i in range(1, amount) if holding[i] < largest] or [i for i in range(1, amount) if holding[i] < reach]
        mass, budget = sum([weights[i] for i in free]), surplus
        for i in free:
            extra = min(reach - holding[i], max(1, budget * weights[i] // mass), surplus)
            holding[i] = holding[i] + extra
            surplus = surplus - extra
    return np.array(holding)


def noise(stream_key, dims, spread, limit, pieces=(), kind=jnp.bfloat16):
    entries = jax.random.normal(stream_key, dims, jnp.float32) * spread
    if len(pieces) > 0:
        entries = shard_levels(stream_key, dims, pieces, -0.22, 0.18) * entries
    return jnp.clip(entries, min=-limit, max=limit).astype(kind)


def setup_inputs(seed: int = 0, part: int = 0) -> dict:
    arg_keys = jax.random.split(jax.random.key(seed), 14)
    part_splits = jax.random.split(jax.random.fold_in(arg_keys[13], part), 14)
    queries = draw_queries(jax.random.fold_in(jax.random.fold_in(arg_keys[13], part), 71), part)
    new_keys = noise(part_splits[1], (SESSIONS, NEW, KVH * HD), 1.0, 4.0, ((0, 4), (2, 4)))
    new_values = noise(part_splits[2], (SESSIONS, NEW, KVH * HD), 1.0, 4.0, ((0, 4), (2, 4)))
    cache_keys = draw_cache_keys(jax.random.fold_in(jax.random.fold_in(arg_keys[13], part), 71), part)
    cache_values = noise(part_splits[4], (SESSIONS, CACHE, KVH * HD), 1.0, 4.0, ((0, 4), (2, 4)))
    cache_len = draw_cache_len(jax.random.fold_in(jax.random.fold_in(arg_keys[13], part), 71), part)
    out_weight = noise(arg_keys[6], (HEADS * HD, D), (16.0 * (HEADS * HD) ** -0.5), 4.0, ((0, 4), (1, 4)))
    residual = noise(part_splits[7], (TOKENS, D), 1.0, 6.0, ((0, 16),), jnp.float32)
    norm_gain = jnp.clip(1.0 + 0.18 * jax.random.normal(arg_keys[8], (D,), jnp.float32), 0.1, 1.9)
    expert_ids_keys = jax.random.split(jax.random.fold_in(part_splits[9], 1), TOKENS // TOK_DEV)
    expert_ids_turns = jax.random.permutation(jax.random.fold_in(part_splits[9], 3), TOKENS // TOK_DEV)
    expert_ids = jax.vmap(lambda own, number: routed_block(jax.random.fold_in(part_splits[9], 2), own, number, TOK_DEV, EXPERTS, TOP, CAP, 2))(expert_ids_keys, expert_ids_turns).reshape((TOKENS, TOP))
    gate_nums = touch_ends(jax.random.randint(part_splits[10], (TOKENS, TOP), 1, 17), jax.random.fold_in(part_splits[10], 1), 1, 16).astype(jnp.int32)
    w_gate_up = noise(arg_keys[11], (EXPERTS, D, 2 * MOE_FF), D ** -0.5, 0.125, ((0, 16),))
    w_down = noise(arg_keys[12], (EXPERTS, MOE_FF, D), MOE_FF ** -0.5, 0.21875, ((0, 16),))
    return {"queries": queries, "new_keys": new_keys, "new_values": new_values, "cache_keys": cache_keys, "cache_values": cache_values, "cache_len": cache_len, "out_weight": out_weight, "residual": residual, "norm_gain": norm_gain, "expert_ids": expert_ids, "gate_nums": gate_nums, "w_gate_up": w_gate_up, "w_down": w_down}


def attend_session(packed):
    q_s, k_new, v_new, k_old, v_old, length = packed
    n_new = q_s.shape[0]
    n_old = k_old.shape[0]
    kv_count = k_old.shape[-1] // HD
    group_size = q_s.shape[-1] // (kv_count * HD)
    q_four = q_s.astype(jnp.float32).reshape(n_new, kv_count, group_size, HD)
    k_old3 = k_old.astype(jnp.float32).reshape(n_old, kv_count, HD)
    v_old3 = v_old.astype(jnp.float32).reshape(n_old, kv_count, HD)
    k_new3 = k_new.astype(jnp.float32).reshape(n_new, kv_count, HD)
    v_new3 = v_new.astype(jnp.float32).reshape(n_new, kv_count, HD)
    scale = 1.0 / HD ** 0.5
    s_old = jnp.einsum('ikgd,jkd->kgij', q_four, k_old3) * scale
    s_new = jnp.einsum('ikgd,jkd->kgij', q_four, k_new3) * scale
    valid_old = jnp.arange(n_old, dtype=jnp.int32) < length
    s_old = jnp.where(valid_old[None, None, None, :], s_old, jnp.float32(-1e+30))
    causal = jnp.arange(n_new, dtype=jnp.int32)[None, :] <= jnp.arange(n_new, dtype=jnp.int32)[:, None]
    s_new = jnp.where(causal[None, None], s_new, jnp.float32(-1e+30))
    top = jnp.maximum(lax.optimization_barrier(jnp.max(s_old, -1, keepdims=True)), lax.optimization_barrier(jnp.max(s_new, -1, keepdims=True)))
    e_old = jnp.exp(s_old - top)
    e_new = jnp.exp(s_new - top)
    total = lax.optimization_barrier(jnp.sum(e_old, -1, keepdims=True)) + lax.optimization_barrier(jnp.sum(e_new, -1, keepdims=True))
    p_old = (e_old / total).astype(jnp.bfloat16).astype(jnp.float32)
    p_new = (e_new / total).astype(jnp.bfloat16).astype(jnp.float32)
    out = jnp.einsum('kgij,jkd->ikgd', p_old, v_old3) + jnp.einsum('kgij,jkd->ikgd', p_new, v_new3)
    return out.reshape(n_new, kv_count * group_size * HD).astype(jnp.bfloat16)

def run_expert(packed):
    block, gate_up, down = packed
    both = jnp.dot(block, gate_up, preferred_element_type=jnp.float32)
    hidden = (jax.nn.silu(both[:, :MOE_FF]) * both[:, MOE_FF:]).astype(jnp.bfloat16)
    return jnp.dot(hidden, down, preferred_element_type=jnp.float32).astype(jnp.bfloat16)

def reference(queries, new_keys, new_values, cache_keys, cache_values, cache_len, out_weight, residual, norm_gain, expert_ids, gate_nums, w_gate_up, w_down):
    attended = lax.map(attend_session, (queries, new_keys, new_values, cache_keys, cache_values, cache_len))
    flat = attended.reshape(TOKENS, HEADS * HD)
    middle = residual + jnp.dot(flat, out_weight, preferred_element_type=jnp.float32)
    meansq = lax.optimization_barrier(jnp.mean(middle * middle, -1, keepdims=True))
    normed = (middle * lax.rsqrt(meansq + 1e-06) * norm_gain).astype(jnp.bfloat16)
    n_dev = N_ATTN * N_EXP
    ids = expert_ids.reshape(n_dev, TOK_DEV * TOP)
    onehot = (ids[:, :, None] == jnp.arange(EXPERTS, dtype=jnp.int32)[None, None, :]).astype(jnp.int32)
    before = jnp.cumsum(onehot, axis=1) - onehot
    slot = lax.optimization_barrier(jnp.sum(before * onehot, -1)).astype(jnp.int32)
    source = jnp.arange(n_dev, dtype=jnp.int32)[:, None]
    index = ((ids * n_dev + source) * CAP + slot).reshape(-1).astype(jnp.int32)
    rows = jnp.broadcast_to(normed.reshape(TOKENS, 1, D), (TOKENS, TOP, D)).reshape(TOKENS * TOP, D)
    buffer = jnp.zeros((EXPERTS * n_dev * CAP, D), jnp.bfloat16).at[index].set(rows)
    outputs = lax.map(run_expert, (buffer.reshape(EXPERTS, n_dev * CAP, D), w_gate_up, w_down))
    picked = outputs.reshape(EXPERTS * n_dev * CAP, D)[index].reshape(TOKENS, TOP, D).astype(jnp.float32)
    numer = gate_nums.astype(jnp.float32)
    weights = numer / lax.optimization_barrier(jnp.sum(numer, -1, keepdims=True))
    return middle + lax.optimization_barrier(jnp.sum(picked * weights[:, :, None], 1))
```

```python
import jax
import jax.numpy as jnp
from jax import lax
from jax.experimental import pallas as pl
from jax.experimental.pallas import tpu as pltpu
from jax.sharding import PartitionSpec as P

HD = 128
LANES = 128
F32 = jnp.float32
BF16 = jnp.bfloat16


def places():
    a = lax.axis_index("attn")
    z = lax.axis_index("exp")
    core = a + 1 - 2 * (a % 2)
    across = (a + 2) % 4
    planes = [z, z + 1 - 2 * (z % 2), (z + 2) % 4, 3 - z]
    return a, z, core, across, planes


def meet(a, z, core, across, planes):
    barrier = pltpu.get_barrier_semaphore()
    peers = [(core, z), (across, z)] + [(a, p) for p in planes[1:]]
    for pa, pz in peers:
        pl.semaphore_signal(
            barrier,
            inc=1,
            device_id={"attn": pa, "exp": pz},
            device_id_type=pl.DeviceIdType.MESH,
        )
    pl.semaphore_wait(barrier, len(peers))


def copy_to(src, dst, sems, i, pa, pz):
    return pltpu.make_async_remote_copy(
        src_ref=src,
        dst_ref=dst,
        send_sem=sems[0].at[i],
        recv_sem=sems[1].at[i],
        device_id={"attn": pa, "exp": pz},
        device_id_type=pl.DeviceIdType.MESH,
    )


def attend(q, k_new, v_new, k_old, v_old, length):
    n_new, n_old = q.shape[0], k_old.shape[0]
    kv_count = k_old.shape[1] // HD
    group = q.shape[1] // (kv_count * HD)
    scale = 1.0 / HD**0.5
    dims = (((1,), (1,)), ((), ()))
    heads = []
    for j in range(kv_count):
        cols = slice(j * HD, (j + 1) * HD)
        rows = jnp.concatenate(
            [q[:, (j * group + g) * HD : (j * group + g + 1) * HD] for g in range(group)], 0
        )
        s_old = lax.dot_general(rows, k_old[:, cols], dims, preferred_element_type=F32) * scale
        s_new = lax.dot_general(rows, k_new[:, cols], dims, preferred_element_type=F32) * scale
        valid = lax.broadcasted_iota(jnp.int32, s_old.shape, 1) < length
        s_old = jnp.where(valid, s_old, F32(-1e30))
        token = lax.broadcasted_iota(jnp.int32, (group, n_new, n_new), 1).reshape(s_new.shape)
        causal = lax.broadcasted_iota(jnp.int32, s_new.shape, 1) <= token
        s_new = jnp.where(causal, s_new, F32(-1e30))
        top = jnp.maximum(jnp.max(s_old, -1, keepdims=True), jnp.max(s_new, -1, keepdims=True))
        e_old = jnp.exp(s_old - top)
        e_new = jnp.exp(s_new - top)
        inv = 1.0 / (jnp.sum(e_old, -1, keepdims=True) + jnp.sum(e_new, -1, keepdims=True))
        p_old = (e_old * inv).astype(BF16)
        p_new = (e_new * inv).astype(BF16)
        out = jnp.dot(p_old, v_old[:, cols], preferred_element_type=F32)
        out = out + jnp.dot(p_new, v_new[:, cols], preferred_element_type=F32)
        out = out.astype(BF16)
        heads += [out[g * n_new : (g + 1) * n_new] for g in range(group)]
    return jnp.concatenate(heads, 1)


def project_kernel(
    len_ref, q_ref, kn_ref, vn_ref, kc_ref, vc_ref, wo_ref, out_ref,
    att, own, csend, crecv, xsend, xrecv, zsend, zrecv, gs, gr, ss, sr,
):
    a, z, core, across, planes = places()
    opposite = (core + 2) % 4
    meet(a, z, core, across, planes)
    g, s = (gs, gr), (ss, sr)
    n_chunk, rows = att.shape[1], att.shape[2]
    n_new = q_ref.shape[1]
    per = rows // n_new
    width = wo_ref.shape[1]

    def chunk_copy(k, j):
        src = att.at[2, j] if k == 3 else att.at[0, j]
        return copy_to(src, att.at[k, j], g, (k - 1) * n_chunk + j, a, planes[2 if k == 2 else 1])

    @pl.loop(0, n_chunk)
    def _(j):
        for i in range(per):
            t = j * per + i
            att[0, j, i * n_new : (i + 1) * n_new, :] = attend(
                q_ref[t], kn_ref[t], vn_ref[t], kc_ref[t], vc_ref[t], len_ref[t]
            )
        chunk_copy(2, j).start()
        chunk_copy(1, j).start()

    def product(k):
        x = jnp.concatenate([att[k, a], att[k, across], att[k, core], att[k, opposite]], 0)
        r = jnp.dot(x, wo_ref[...], preferred_element_type=F32)
        own[k] = r[: 2 * rows]
        csend[k] = r[2 * rows :]
        core_copy(k).start()

    def core_copy(k):
        return copy_to(csend.at[k], crecv.at[k], s, k, core, z)

    def x_copy(k):
        return copy_to(xsend.at[k], xrecv.at[k], s, 4 + k, across, z)

    def z_copy(k):
        return copy_to(zsend.at[k - 1], zrecv.at[k - 1], s, 7 + k, a, planes[k])

    def to_x(k):
        core_copy(k).wait_recv()
        xsend[k] = own[k, rows:, :] + crecv[k, rows:, :]
        x_copy(k).start()

    def to_z(k):
        x_copy(k).wait_recv()
        total = own[k, :rows, :] + crecv[k, :rows, :] + xrecv[k]
        if k == 0:
            out_ref[:, pl.ds(pl.multiple_of(z * width, LANES), width)] = total
        else:
            zsend[k - 1] = total
            z_copy(k).start()

    @pl.loop(0, n_chunk)
    def _(j):
        chunk_copy(2, j).wait_recv()
        chunk_copy(3, j).start()

    product(0)
    for j in range(n_chunk):
        chunk_copy(1, j).wait_recv()
    product(1)
    to_x(0)
    product(2)
    to_x(1)
    to_z(0)
    to_x(2)
    to_z(1)
    to_z(2)
    for j in range(n_chunk):
        chunk_copy(3, j).wait_recv()
    product(3)
    to_x(3)
    to_z(3)
    for k in range(1, 4):
        z_copy(k).wait_recv()
        out_ref[:, pl.ds(pl.multiple_of(planes[k] * width, LANES), width)] = zrecv[k - 1]

    @pl.loop(0, n_chunk)
    def _(j):
        for k in range(1, 4):
            chunk_copy(k, j).wait_send()

    for k in range(4):
        core_copy(k).wait_send()
        x_copy(k).wait_send()
        if k > 0:
            z_copy(k).wait_send()


def project(queries, new_keys, new_values, cache_keys, cache_values, cache_len, out_weight):
    sessions, n_new, width = queries.shape
    rows = sessions * n_new // 4
    cols = out_weight.shape[1]
    vmem = pl.BlockSpec(memory_space=pltpu.VMEM)
    return pl.pallas_call(
        project_kernel,
        out_shape=jax.ShapeDtypeStruct((rows, 4 * cols), F32),
        in_specs=[pl.BlockSpec(memory_space=pltpu.SMEM)] + [vmem] * 6,
        out_specs=vmem,
        scratch_shapes=[
            pltpu.VMEM((4, 4, rows, width), BF16),
            pltpu.VMEM((4, 2 * rows, cols), F32),
            pltpu.VMEM((4, 2 * rows, cols), F32),
            pltpu.VMEM((4, 2 * rows, cols), F32),
            pltpu.VMEM((4, rows, cols), F32),
            pltpu.VMEM((4, rows, cols), F32),
            pltpu.VMEM((3, rows, cols), F32),
            pltpu.VMEM((3, rows, cols), F32),
            pltpu.SemaphoreType.DMA((12,)),
            pltpu.SemaphoreType.DMA((12,)),
            pltpu.SemaphoreType.DMA((11,)),
            pltpu.SemaphoreType.DMA((11,)),
        ],
        compiler_params=pltpu.CompilerParams(
            collective_id=0, has_side_effects=True, vmem_limit_bytes=40 << 20
        ),
    )(cache_len, queries, new_keys, new_values, cache_keys, cache_values, out_weight)


def experts_kernel(
    pay_ref, wgu_hbm, wd_hbm, out_ref,
    wgu, wd, xall, hid, own, csend, crecv, xsend, xrecv, zsend, zrecv, wsem, gs, gr, ss, sr,
):
    a, z, core, across, planes = places()
    load_gu = pltpu.make_async_copy(wgu_hbm.at[0], wgu, wsem.at[0])
    load_d = pltpu.make_async_copy(wd_hbm.at[0], wd, wsem.at[1])
    load_gu.start()
    load_d.start()
    meet(a, z, core, across, planes)
    g, s = (gs, gr), (ss, sr)
    rows, width = out_ref.shape
    units = wd.shape[0]
    mine = a * 4 + z

    def z_in(k):
        src = xall.at[2, 0] if k == 3 else xall.at[0, 0]
        return copy_to(src, xall.at[k, 0], g, k - 1, a, planes[2 if k == 2 else 1])

    def x_in(k):
        return copy_to(xall.at[k, 0], xall.at[k, 1], g, 3 + k, across, z)

    def core_in(k, i):
        return copy_to(xall.at[k, i], xall.at[k, 2 + i], g, 7 + 2 * k + i, core, z)

    def core_copy(k):
        return copy_to(csend.at[k], crecv.at[k], s, k, core, z)

    def x_copy(k):
        return copy_to(xsend.at[k], xrecv.at[k], s, 4 + k, across, z)

    def z_copy(k):
        return copy_to(zsend.at[k - 1], zrecv.at[k - 1], s, 7 + k, a, planes[k])

    def compute(k):
        core_in(k, 0).wait_recv()
        core_in(k, 1).wait_recv()
        if k == 0:
            load_gu.wait()
        x = xall[k].reshape(4 * rows, width + LANES)[:, :width]
        nums = xall[k].reshape(4 * rows, width + LANES)[:, width:].astype(F32)
        lane = lax.broadcasted_iota(jnp.int32, nums.shape, 1)
        num = jnp.sum(jnp.where(lane == mine, nums, F32(0)), -1, keepdims=True)
        weight = num / jnp.sum(nums, -1, keepdims=True)

        @pl.loop(0, units // 256)
        def _(t):
            at = pl.multiple_of(t * 256, 256)
            gate = jnp.dot(x, wgu[:, pl.ds(at, 256)], preferred_element_type=F32)
            up = jnp.dot(
                x,
                wgu[:, pl.ds(pl.multiple_of(units + t * 256, 256), 256)],
                preferred_element_type=F32,
            )
            hid[:, pl.ds(at, 256)] = (gate / (1.0 + jnp.exp(-gate)) * up).astype(BF16)

        if k == 0:
            load_d.wait()

        @pl.loop(0, width // 512)
        def _(t):
            at = pl.ds(pl.multiple_of(t * 512, 512), 512)
            r = jnp.dot(hid[...], wd[:, at], preferred_element_type=F32) * weight
            own[k, :, at] = r[: 2 * rows]
            csend[k, :, at] = r[2 * rows :].astype(BF16)

        core_copy(k).start()

    def to_x(k):
        core_copy(k).wait_recv()
        xsend[k] = (own[k, rows:, :] + crecv[k, rows:, :].astype(F32)).astype(BF16)
        x_copy(k).start()

    def to_z(k):
        x_copy(k).wait_recv()
        total = own[k, :rows, :] + crecv[k, :rows, :].astype(F32) + xrecv[k].astype(F32)
        if k == 0:
            out_ref[...] = total
        else:
            zsend[k - 1] = total.astype(BF16)
            z_copy(k).start()

    xall[0, 0] = pay_ref[...]
    z_in(2).start()
    z_in(1).start()
    x_in(0).start()
    core_in(0, 0).start()

    def pass_z(k):
        z_in(k).wait_recv()
        if k == 2:
            z_in(3).start()
        x_in(k).start()
        core_in(k, 0).start()

    def pass_x(k):
        x_in(k).wait_recv()
        core_in(k, 1).start()

    pass_x(0)
    pass_z(1)
    pass_z(2)
    compute(0)
    pass_x(1)
    pass_z(3)
    to_x(0)
    compute(1)
    pass_x(2)
    to_x(1)
    to_z(0)
    compute(2)
    pass_x(3)
    to_x(2)
    to_z(1)
    compute(3)
    to_z(2)
    to_x(3)
    to_z(3)
    for k in range(1, 4):
        z_copy(k).wait_recv()
    out_ref[...] += zrecv[0].astype(F32) + zrecv[1].astype(F32) + zrecv[2].astype(F32)
    for k in range(4):
        x_in(k).wait_send()
        core_in(k, 0).wait_send()
        core_in(k, 1).wait_send()
        core_copy(k).wait_send()
        x_copy(k).wait_send()
        if k > 0:
            z_in(k).wait_send()
            z_copy(k).wait_send()


def experts(payload, w_gate_up, w_down):
    rows = payload.shape[0]
    width = payload.shape[1] - LANES
    units = w_down.shape[1]
    vmem = pl.BlockSpec(memory_space=pltpu.VMEM)
    hbm = pl.BlockSpec(memory_space=pl.ANY)
    return pl.pallas_call(
        experts_kernel,
        out_shape=jax.ShapeDtypeStruct((rows, width), F32),
        in_specs=[vmem, hbm, hbm],
        out_specs=vmem,
        scratch_shapes=[
            pltpu.VMEM((width, 2 * units), BF16),
            pltpu.VMEM((units, width), BF16),
            pltpu.VMEM((4, 4, rows, width + LANES), BF16),
            pltpu.VMEM((4 * rows, units), BF16),
            pltpu.VMEM((4, 2 * rows, width), F32),
            pltpu.VMEM((4, 2 * rows, width), BF16),
            pltpu.VMEM((4, 2 * rows, width), BF16),
            pltpu.VMEM((4, rows, width), BF16),
            pltpu.VMEM((4, rows, width), BF16),
            pltpu.VMEM((3, rows, width), BF16),
            pltpu.VMEM((3, rows, width), BF16),
            pltpu.SemaphoreType.DMA((2,)),
            pltpu.SemaphoreType.DMA((15,)),
            pltpu.SemaphoreType.DMA((15,)),
            pltpu.SemaphoreType.DMA((11,)),
            pltpu.SemaphoreType.DMA((11,)),
        ],
        compiler_params=pltpu.CompilerParams(
            collective_id=1, has_side_effects=True, vmem_limit_bytes=48 << 20
        ),
    )(payload, w_gate_up, w_down)


def grid_shards(
    queries,
    new_keys,
    new_values,
    cache_keys,
    cache_values,
    cache_len,
    out_weight,
    residual,
    norm_gain,
    expert_ids,
    gate_nums,
    w_gate_up,
    w_down,
):
    projected = project(
        queries, new_keys, new_values, cache_keys, cache_values, cache_len, out_weight
    )
    middle = residual + projected
    meansq = jnp.mean(middle * middle, -1, keepdims=True)
    normed = (middle * lax.rsqrt(meansq + 1e-06) * norm_gain).astype(BF16)
    chosen = expert_ids[:, :, None] == jnp.arange(LANES, dtype=jnp.int32)[None, None, :]
    nums = jnp.sum(jnp.where(chosen, gate_nums[:, :, None], 0), 1).astype(BF16)
    payload = jnp.concatenate([normed, nums], 1)
    return middle + experts(payload, w_gate_up, w_down)


def attend_session(packed):
    q_s, k_new, v_new, k_old, v_old, length = packed
    n_new = q_s.shape[0]
    n_old = k_old.shape[0]
    kv_count = k_old.shape[-1] // HD
    group_size = q_s.shape[-1] // (kv_count * HD)
    q_four = q_s.reshape(n_new, kv_count, group_size, HD)
    k_old3 = k_old.reshape(n_old, kv_count, HD)
    v_old3 = v_old.reshape(n_old, kv_count, HD)
    k_new3 = k_new.reshape(n_new, kv_count, HD)
    v_new3 = v_new.reshape(n_new, kv_count, HD)
    scale = 1.0 / HD**0.5
    s_old = jnp.einsum("ikgd,jkd->kgij", q_four, k_old3, preferred_element_type=jnp.float32) * scale
    s_new = jnp.einsum("ikgd,jkd->kgij", q_four, k_new3, preferred_element_type=jnp.float32) * scale
    valid_old = jnp.arange(n_old, dtype=jnp.int32) < length
    s_old = jnp.where(valid_old[None, None, None, :], s_old, jnp.float32(-1e30))
    causal = (
        jnp.arange(n_new, dtype=jnp.int32)[None, :] <= jnp.arange(n_new, dtype=jnp.int32)[:, None]
    )
    s_new = jnp.where(causal[None, None], s_new, jnp.float32(-1e30))
    top = jnp.maximum(jnp.max(s_old, -1, keepdims=True), jnp.max(s_new, -1, keepdims=True))
    e_old = jnp.exp(s_old - top)
    e_new = jnp.exp(s_new - top)
    total = jnp.sum(e_old, -1, keepdims=True) + jnp.sum(e_new, -1, keepdims=True)
    p_old = (e_old / total).astype(jnp.bfloat16)
    p_new = (e_new / total).astype(jnp.bfloat16)
    out = jnp.einsum("kgij,jkd->ikgd", p_old, v_old3, preferred_element_type=jnp.float32)
    out = out + jnp.einsum("kgij,jkd->ikgd", p_new, v_new3, preferred_element_type=jnp.float32)
    return out.reshape(n_new, kv_count * group_size * HD).astype(jnp.bfloat16)


def shards(
    queries,
    new_keys,
    new_values,
    cache_keys,
    cache_values,
    cache_len,
    out_weight,
    residual,
    norm_gain,
    expert_ids,
    gate_nums,
    w_gate_up,
    w_down,
):
    attended = lax.map(
        attend_session, (queries, new_keys, new_values, cache_keys, cache_values, cache_len)
    )
    local_rows = attended.reshape(attended.shape[0] * attended.shape[1], attended.shape[2])
    spread = jnp.dot(
        lax.all_gather(local_rows, "exp", axis=0, tiled=True),
        out_weight,
        preferred_element_type=jnp.float32,
    )
    partial_value = lax.all_to_all(spread, "exp", split_axis=0, concat_axis=1, tiled=True)
    projected = lax.psum_scatter(partial_value, "attn", scatter_dimension=0, tiled=True)
    middle = residual + projected
    meansq = jnp.mean(middle * middle, -1, keepdims=True)
    normed = (middle * lax.rsqrt(meansq + 1e-06) * norm_gain).astype(jnp.bfloat16)
    tok_rows = expert_ids.shape[0]
    top_count = expert_ids.shape[1]
    exp_dev = w_gate_up.shape[0]
    hidden_units = w_down.shape[1]
    n_experts = exp_dev * lax.axis_size("attn") * lax.axis_size("exp")
    capacity = max(2, 2 * tok_rows * top_count // n_experts)
    flat_ids = expert_ids.reshape(-1)
    onehot = (flat_ids[:, None] == jnp.arange(n_experts, dtype=jnp.int32)[None, :]).astype(
        jnp.int32
    )
    before = jnp.cumsum(onehot, axis=0) - onehot
    slot = jnp.sum(before * onehot, -1)
    target = (flat_ids * capacity + slot).reshape(tok_rows, top_count)
    places = jnp.arange(n_experts * capacity, dtype=jnp.int32)
    placing = jnp.sum((places[:, None, None] == target[None, :, :]).astype(jnp.int32), -1).astype(
        jnp.bfloat16
    )
    sent = jnp.dot(placing, normed, preferred_element_type=jnp.float32).astype(jnp.bfloat16)
    sent = sent.reshape(n_experts, capacity, normed.shape[1])
    block = lax.all_to_all(sent, ("attn", "exp"), split_axis=0, concat_axis=0, tiled=True)
    n_src = block.shape[0] // exp_dev
    rows_four = block.reshape(n_src, exp_dev, block.shape[1], block.shape[2])
    both = jnp.einsum("sjmd,jdf->sjmf", rows_four, w_gate_up, preferred_element_type=jnp.float32)
    hidden = (jax.nn.silu(both[..., :hidden_units]) * both[..., hidden_units:]).astype(jnp.bfloat16)
    result = jnp.einsum("sjmf,jfd->sjmd", hidden, w_down, preferred_element_type=jnp.float32)
    result = result.astype(jnp.bfloat16).reshape(block.shape)
    returned = lax.all_to_all(result, ("attn", "exp"), split_axis=0, concat_axis=0, tiled=True)
    picked = (
        returned[flat_ids, slot].reshape(tok_rows, top_count, normed.shape[1]).astype(jnp.float32)
    )
    numer = gate_nums.astype(jnp.float32)
    weights = numer / jnp.sum(numer, -1, keepdims=True)
    return middle + jnp.sum(picked * weights[:, :, None], 1)


def fits_grid(mesh):
    return mesh.shape["attn"] == 4 and mesh.shape["exp"] == 4


def solution(mesh):
    in_specs = (
        P(("groups", "exp"), None, "attn"),
        P(("groups", "exp"), None, "attn"),
        P(("groups", "exp"), None, "attn"),
        P(("groups", "exp"), None, "attn"),
        P(("groups", "exp"), None, "attn"),
        P(("groups", "exp")),
        P("attn", "exp"),
        P(("groups", "exp", "attn"), None),
        P(),
        P(("groups", "exp", "attn"), None),
        P(("groups", "exp", "attn"), None),
        P(("attn", "exp"), None, None),
        P(("attn", "exp"), None, None),
    )
    out_specs = P(("groups", "exp", "attn"), None)
    body = grid_shards if fits_grid(mesh) else shards
    return jax.shard_map(body, mesh=mesh, in_specs=in_specs, out_specs=out_specs, check_vma=False)
```

```python
import jax
import jax.numpy as jnp
from jax import lax
from jax.experimental import pallas as pl
from jax.experimental.pallas import tpu as pltpu
from jax.sharding import PartitionSpec as P

HD = 128
LANES = 128
F32 = jnp.float32
BF16 = jnp.bfloat16


def places():
    a = lax.axis_index("attn")
    z = lax.axis_index("exp")
    core = a + 1 - 2 * (a % 2)
    across = (a + 2) % 4
    planes = [z, z + 1 - 2 * (z % 2), (z + 2) % 4, 3 - z]
    return a, z, core, across, planes


def meet(a, z, core, across, planes):
    barrier = pltpu.get_barrier_semaphore()
    peers = [(core, z), (across, z)] + [(a, p) for p in planes[1:]]
    for pa, pz in peers:
        pl.semaphore_signal(
            barrier,
            inc=1,
            device_id={"attn": pa, "exp": pz},
            device_id_type=pl.DeviceIdType.MESH,
        )
    pl.semaphore_wait(barrier, len(peers))


def copy_to(src, dst, sems, i, pa, pz):
    return pltpu.make_async_remote_copy(
        src_ref=src,
        dst_ref=dst,
        send_sem=sems[0].at[i],
        recv_sem=sems[1].at[i],
        device_id={"attn": pa, "exp": pz},
        device_id_type=pl.DeviceIdType.MESH,
    )


def attend(q, k_new, v_new, k_old, v_old, length):
    n_new, n_old = q.shape[0], k_old.shape[0]
    kv_count = k_old.shape[1] // HD
    group = q.shape[1] // (kv_count * HD)
    scale = 1.0 / HD**0.5
    dims = (((1,), (1,)), ((), ()))
    heads = []
    for j in range(kv_count):
        cols = slice(j * HD, (j + 1) * HD)
        rows = jnp.concatenate(
            [q[:, (j * group + g) * HD : (j * group + g + 1) * HD] for g in range(group)], 0
        )
        s_old = lax.dot_general(rows, k_old[:, cols], dims, preferred_element_type=F32) * scale
        s_new = lax.dot_general(rows, k_new[:, cols], dims, preferred_element_type=F32) * scale
        valid = lax.broadcasted_iota(jnp.int32, s_old.shape, 1) < length
        s_old = jnp.where(valid, s_old, F32(-1e30))
        token = lax.broadcasted_iota(jnp.int32, (group, n_new, n_new), 1).reshape(s_new.shape)
        causal = lax.broadcasted_iota(jnp.int32, s_new.shape, 1) <= token
        s_new = jnp.where(causal, s_new, F32(-1e30))
        top = jnp.maximum(jnp.max(s_old, -1, keepdims=True), jnp.max(s_new, -1, keepdims=True))
        e_old = jnp.exp(s_old - top)
        e_new = jnp.exp(s_new - top)
        inv = 1.0 / (jnp.sum(e_old, -1, keepdims=True) + jnp.sum(e_new, -1, keepdims=True))
        p_old = (e_old * inv).astype(BF16)
        p_new = (e_new * inv).astype(BF16)
        out = jnp.dot(p_old, v_old[:, cols], preferred_element_type=F32)
        out = out + jnp.dot(p_new, v_new[:, cols], preferred_element_type=F32)
        out = out.astype(BF16)
        heads += [out[g * n_new : (g + 1) * n_new] for g in range(group)]
    return jnp.concatenate(heads, 1)


def project_kernel(
    len_ref, q_hbm, kn_hbm, vn_hbm, kc_hbm, vc_hbm, wo_hbm, out_ref,
    q_ref, kn_ref, vn_ref, kc_ref, vc_ref, wo_ref, lsem, att, own, csend, crecv, xsend, xrecv, zsend, zrecv, gs, gr, ss, sr,
):
    a, z, core, across, planes = places()
    opposite = (core + 2) % 4
    loads = [
        pltpu.make_async_copy(src, dst, lsem.at[i])
        for i, (src, dst) in enumerate(
            [
                (q_hbm, q_ref),
                (kn_hbm, kn_ref),
                (vn_hbm, vn_ref),
                (kc_hbm, kc_ref),
                (vc_hbm, vc_ref),
                (wo_hbm, wo_ref),
            ]
        )
    ]
    for load in loads:
        load.start()
    meet(a, z, core, across, planes)
    for load in loads:
        load.wait()
    g, s = (gs, gr), (ss, sr)
    n_chunk, rows = att.shape[1], att.shape[2]
    n_new = q_ref.shape[1]
    per = rows // n_new
    width = wo_ref.shape[1]

    def chunk_copy(k, j):
        src = att.at[2, j] if k == 3 else att.at[0, j]
        return copy_to(src, att.at[k, j], g, (k - 1) * n_chunk + j, a, planes[2 if k == 2 else 1])

    @pl.loop(0, n_chunk)
    def _(j):
        for i in range(per):
            t = j * per + i
            att[0, j, i * n_new : (i + 1) * n_new, :] = attend(
                q_ref[t], kn_ref[t], vn_ref[t], kc_ref[t], vc_ref[t], len_ref[t]
            )
        chunk_copy(2, j).start()
        chunk_copy(1, j).start()

    def product(k):
        x = jnp.concatenate([att[k, a], att[k, across], att[k, core], att[k, opposite]], 0)
        r = jnp.dot(x, wo_ref[...], preferred_element_type=F32)
        own[k] = r[: 2 * rows]
        csend[k] = r[2 * rows :]
        core_copy(k).start()

    def core_copy(k):
        return copy_to(csend.at[k], crecv.at[k], s, k, core, z)

    def x_copy(k):
        return copy_to(xsend.at[k], xrecv.at[k], s, 4 + k, across, z)

    def z_copy(k):
        return copy_to(zsend.at[k - 1], zrecv.at[k - 1], s, 7 + k, a, planes[k])

    def to_x(k):
        core_copy(k).wait_recv()
        xsend[k] = (own[k, rows:, :] + crecv[k, rows:, :]).astype(BF16)
        x_copy(k).start()

    def to_z(k):
        x_copy(k).wait_recv()
        total = own[k, :rows, :] + crecv[k, :rows, :] + xrecv[k].astype(F32)
        if k == 0:
            out_ref[:, pl.ds(pl.multiple_of(z * width, LANES), width)] = total
        else:
            zsend[k - 1] = total.astype(BF16)
            z_copy(k).start()

    @pl.loop(0, n_chunk)
    def _(j):
        chunk_copy(2, j).wait_recv()
        chunk_copy(3, j).start()

    product(0)
    for j in range(n_chunk):
        chunk_copy(1, j).wait_recv()
    product(1)
    to_x(0)
    product(2)
    to_x(1)
    to_z(0)
    to_x(2)
    to_z(1)
    to_z(2)
    for j in range(n_chunk):
        chunk_copy(3, j).wait_recv()
    product(3)
    to_x(3)
    to_z(3)
    for k in range(1, 4):
        z_copy(k).wait_recv()
        out_ref[:, pl.ds(pl.multiple_of(planes[k] * width, LANES), width)] = zrecv[k - 1].astype(F32)

    @pl.loop(0, n_chunk)
    def _(j):
        for k in range(1, 4):
            chunk_copy(k, j).wait_send()

    for k in range(4):
        core_copy(k).wait_send()
        x_copy(k).wait_send()
        if k > 0:
            z_copy(k).wait_send()


def project(queries, new_keys, new_values, cache_keys, cache_values, cache_len, out_weight):
    sessions, n_new, width = queries.shape
    rows = sessions * n_new // 4
    cols = out_weight.shape[1]
    vmem = pl.BlockSpec(memory_space=pltpu.VMEM)
    return pl.pallas_call(
        project_kernel,
        out_shape=jax.ShapeDtypeStruct((rows, 4 * cols), F32),
        in_specs=[pl.BlockSpec(memory_space=pltpu.SMEM)] + [pl.BlockSpec(memory_space=pl.ANY)] * 6,
        out_specs=vmem,
        scratch_shapes=[
            pltpu.VMEM(queries.shape, BF16),
            pltpu.VMEM(new_keys.shape, BF16),
            pltpu.VMEM(new_values.shape, BF16),
            pltpu.VMEM(cache_keys.shape, BF16),
            pltpu.VMEM(cache_values.shape, BF16),
            pltpu.VMEM(out_weight.shape, BF16),
            pltpu.SemaphoreType.DMA((6,)),
            pltpu.VMEM((4, 4, rows, width), BF16),
            pltpu.VMEM((4, 2 * rows, cols), F32),
            pltpu.VMEM((4, 2 * rows, cols), F32),
            pltpu.VMEM((4, 2 * rows, cols), F32),
            pltpu.VMEM((4, rows, cols), BF16),
            pltpu.VMEM((4, rows, cols), BF16),
            pltpu.VMEM((3, rows, cols), BF16),
            pltpu.VMEM((3, rows, cols), BF16),
            pltpu.SemaphoreType.DMA((12,)),
            pltpu.SemaphoreType.DMA((12,)),
            pltpu.SemaphoreType.DMA((11,)),
            pltpu.SemaphoreType.DMA((11,)),
        ],
        compiler_params=pltpu.CompilerParams(
            collective_id=0, has_side_effects=True, vmem_limit_bytes=56 << 20
        ),
    )(cache_len, queries, new_keys, new_values, cache_keys, cache_values, out_weight)


def experts_kernel(
    pay_ref, wgu_hbm, wd_hbm, out_ref,
    wgu, wd, xall, hid, own, csend, crecv, xsend, xrecv, zsend, zrecv, wsem, gs, gr, ss, sr,
):
    a, z, core, across, planes = places()
    load_gu = pltpu.make_async_copy(wgu_hbm.at[0], wgu, wsem.at[0])
    load_d = pltpu.make_async_copy(wd_hbm.at[0], wd, wsem.at[1])
    load_gu.start()
    load_d.start()
    meet(a, z, core, across, planes)
    g, s = (gs, gr), (ss, sr)
    rows, width = out_ref.shape
    units = wd.shape[0]
    mine = a * 4 + z

    def z_in(k):
        src = xall.at[2, 0] if k == 3 else xall.at[0, 0]
        return copy_to(src, xall.at[k, 0], g, k - 1, a, planes[2 if k == 2 else 1])

    def x_in(k):
        if k == 1:
            return copy_to(xall.at[0, 1], xall.at[1, 1], g, 4, a, planes[1])
        return copy_to(xall.at[k, 0], xall.at[k, 1], g, 3 + k, across, z)

    def core_in(k, i):
        return copy_to(xall.at[k, i], xall.at[k, 2 + i], g, 7 + 2 * k + i, core, z)

    def core_copy(k):
        return copy_to(csend.at[k], crecv.at[k], s, k, core, z)

    def x_copy(k):
        return copy_to(xsend.at[k], xrecv.at[k], s, 4 + k, across, z)

    def z_copy(k):
        return copy_to(zsend.at[k - 1], zrecv.at[k - 1], s, 7 + k, a, planes[k])

    def compute(k):
        core_in(k, 0).wait_recv()
        core_in(k, 1).wait_recv()
        if k == 0:
            load_gu.wait()
        x = xall[k].reshape(4 * rows, width + LANES)[:, :width]
        nums = xall[k].reshape(4 * rows, width + LANES)[:, width:].astype(F32)
        lane = lax.broadcasted_iota(jnp.int32, nums.shape, 1)
        num = jnp.sum(jnp.where(lane == mine, nums, F32(0)), -1, keepdims=True)
        weight = num / jnp.sum(nums, -1, keepdims=True)

        @pl.loop(0, units // 256)
        def _(t):
            at = pl.multiple_of(t * 256, 256)
            gate = jnp.dot(x, wgu[:, pl.ds(at, 256)], preferred_element_type=F32)
            up = jnp.dot(
                x,
                wgu[:, pl.ds(pl.multiple_of(units + t * 256, 256), 256)],
                preferred_element_type=F32,
            )
            hid[:, pl.ds(at, 256)] = (gate / (1.0 + jnp.exp(-gate)) * up).astype(BF16)

        if k == 0:
            load_d.wait()

        @pl.loop(0, width // 512)
        def _(t):
            at = pl.ds(pl.multiple_of(t * 512, 512), 512)
            r = jnp.dot(hid[...], wd[:, at], preferred_element_type=F32) * weight
            own[k, :, at] = r[: 2 * rows]
            csend[k, :, at] = r[2 * rows :].astype(BF16)

        core_copy(k).start()

    def to_x(k):
        core_copy(k).wait_recv()
        xsend[k] = (own[k, rows:, :] + crecv[k, rows:, :].astype(F32)).astype(BF16)
        x_copy(k).start()

    def to_z(k):
        x_copy(k).wait_recv()
        total = own[k, :rows, :] + crecv[k, :rows, :].astype(F32) + xrecv[k].astype(F32)
        if k == 0:
            out_ref[...] = total
        else:
            zsend[k - 1] = total.astype(BF16)
            z_copy(k).start()

    xall[0, 0] = pay_ref[...]
    z_in(2).start()
    z_in(1).start()
    x_in(0).start()
    core_in(0, 0).start()

    def pass_z(k):
        z_in(k).wait_recv()
        if k == 2:
            z_in(3).start()
        if k != 1:
            x_in(k).start()
        core_in(k, 0).start()

    def pass_x(k):
        x_in(k).wait_recv()
        if k == 0:
            x_in(1).start()
        core_in(k, 1).start()

    pass_x(0)
    pass_z(1)
    pass_z(2)
    pass_x(1)
    compute(0)
    pass_z(3)
    compute(1)
    pass_x(2)
    to_x(1)
    pass_x(3)
    compute(2)
    to_x(2)
    to_z(1)
    compute(3)
    to_x(3)
    to_x(0)
    to_z(2)
    to_z(3)
    to_z(0)
    for k in range(1, 4):
        z_copy(k).wait_recv()
    out_ref[...] += zrecv[0].astype(F32) + zrecv[1].astype(F32) + zrecv[2].astype(F32)
    for k in range(4):
        x_in(k).wait_send()
        core_in(k, 0).wait_send()
        core_in(k, 1).wait_send()
        core_copy(k).wait_send()
        x_copy(k).wait_send()
        if k > 0:
            z_in(k).wait_send()
            z_copy(k).wait_send()


def experts(payload, w_gate_up, w_down):
    rows = payload.shape[0]
    width = payload.shape[1] - LANES
    units = w_down.shape[1]
    vmem = pl.BlockSpec(memory_space=pltpu.VMEM)
    hbm = pl.BlockSpec(memory_space=pl.ANY)
    return pl.pallas_call(
        experts_kernel,
        out_shape=jax.ShapeDtypeStruct((rows, width), F32),
        in_specs=[vmem, hbm, hbm],
        out_specs=vmem,
        scratch_shapes=[
            pltpu.VMEM((width, 2 * units), BF16),
            pltpu.VMEM((units, width), BF16),
            pltpu.VMEM((4, 4, rows, width + LANES), BF16),
            pltpu.VMEM((4 * rows, units), BF16),
            pltpu.VMEM((4, 2 * rows, width), F32),
            pltpu.VMEM((4, 2 * rows, width), BF16),
            pltpu.VMEM((4, 2 * rows, width), BF16),
            pltpu.VMEM((4, rows, width), BF16),
            pltpu.VMEM((4, rows, width), BF16),
            pltpu.VMEM((3, rows, width), BF16),
            pltpu.VMEM((3, rows, width), BF16),
            pltpu.SemaphoreType.DMA((2,)),
            pltpu.SemaphoreType.DMA((15,)),
            pltpu.SemaphoreType.DMA((15,)),
            pltpu.SemaphoreType.DMA((11,)),
            pltpu.SemaphoreType.DMA((11,)),
        ],
        compiler_params=pltpu.CompilerParams(
            collective_id=1, has_side_effects=True, vmem_limit_bytes=48 << 20
        ),
    )(payload, w_gate_up, w_down)


def grid_shards(
    queries,
    new_keys,
    new_values,
    cache_keys,
    cache_values,
    cache_len,
    out_weight,
    residual,
    norm_gain,
    expert_ids,
    gate_nums,
    w_gate_up,
    w_down,
):
    projected = project(
        queries, new_keys, new_values, cache_keys, cache_values, cache_len, out_weight
    )
    middle = residual + projected
    meansq = jnp.mean(middle * middle, -1, keepdims=True)
    normed = (middle * lax.rsqrt(meansq + 1e-06) * norm_gain).astype(BF16)
    chosen = expert_ids[:, :, None] == jnp.arange(LANES, dtype=jnp.int32)[None, None, :]
    nums = jnp.sum(jnp.where(chosen, gate_nums[:, :, None], 0), 1).astype(BF16)
    payload = jnp.concatenate([normed, nums], 1)
    return middle + experts(payload, w_gate_up, w_down)


def attend_session(packed):
    q_s, k_new, v_new, k_old, v_old, length = packed
    n_new = q_s.shape[0]
    n_old = k_old.shape[0]
    kv_count = k_old.shape[-1] // HD
    group_size = q_s.shape[-1] // (kv_count * HD)
    q_four = q_s.reshape(n_new, kv_count, group_size, HD)
    k_old3 = k_old.reshape(n_old, kv_count, HD)
    v_old3 = v_old.reshape(n_old, kv_count, HD)
    k_new3 = k_new.reshape(n_new, kv_count, HD)
    v_new3 = v_new.reshape(n_new, kv_count, HD)
    scale = 1.0 / HD**0.5
    s_old = jnp.einsum("ikgd,jkd->kgij", q_four, k_old3, preferred_element_type=jnp.float32) * scale
    s_new = jnp.einsum("ikgd,jkd->kgij", q_four, k_new3, preferred_element_type=jnp.float32) * scale
    valid_old = jnp.arange(n_old, dtype=jnp.int32) < length
    s_old = jnp.where(valid_old[None, None, None, :], s_old, jnp.float32(-1e30))
    causal = (
        jnp.arange(n_new, dtype=jnp.int32)[None, :] <= jnp.arange(n_new, dtype=jnp.int32)[:, None]
    )
    s_new = jnp.where(causal[None, None], s_new, jnp.float32(-1e30))
    top = jnp.maximum(jnp.max(s_old, -1, keepdims=True), jnp.max(s_new, -1, keepdims=True))
    e_old = jnp.exp(s_old - top)
    e_new = jnp.exp(s_new - top)
    total = jnp.sum(e_old, -1, keepdims=True) + jnp.sum(e_new, -1, keepdims=True)
    p_old = (e_old / total).astype(jnp.bfloat16)
    p_new = (e_new / total).astype(jnp.bfloat16)
    out = jnp.einsum("kgij,jkd->ikgd", p_old, v_old3, preferred_element_type=jnp.float32)
    out = out + jnp.einsum("kgij,jkd->ikgd", p_new, v_new3, preferred_element_type=jnp.float32)
    return out.reshape(n_new, kv_count * group_size * HD).astype(jnp.bfloat16)


def shards(
    queries,
    new_keys,
    new_values,
    cache_keys,
    cache_values,
    cache_len,
    out_weight,
    residual,
    norm_gain,
    expert_ids,
    gate_nums,
    w_gate_up,
    w_down,
):
    attended = lax.map(
        attend_session, (queries, new_keys, new_values, cache_keys, cache_values, cache_len)
    )
    local_rows = attended.reshape(attended.shape[0] * attended.shape[1], attended.shape[2])
    spread = jnp.dot(
        lax.all_gather(local_rows, "exp", axis=0, tiled=True),
        out_weight,
        preferred_element_type=jnp.float32,
    )
    partial_value = lax.all_to_all(spread, "exp", split_axis=0, concat_axis=1, tiled=True)
    projected = lax.psum_scatter(partial_value, "attn", scatter_dimension=0, tiled=True)
    middle = residual + projected
    meansq = jnp.mean(middle * middle, -1, keepdims=True)
    normed = (middle * lax.rsqrt(meansq + 1e-06) * norm_gain).astype(jnp.bfloat16)
    tok_rows = expert_ids.shape[0]
    top_count = expert_ids.shape[1]
    exp_dev = w_gate_up.shape[0]
    hidden_units = w_down.shape[1]
    n_experts = exp_dev * lax.axis_size("attn") * lax.axis_size("exp")
    capacity = max(2, 2 * tok_rows * top_count // n_experts)
    flat_ids = expert_ids.reshape(-1)
    onehot = (flat_ids[:, None] == jnp.arange(n_experts, dtype=jnp.int32)[None, :]).astype(
        jnp.int32
    )
    before = jnp.cumsum(onehot, axis=0) - onehot
    slot = jnp.sum(before * onehot, -1)
    target = (flat_ids * capacity + slot).reshape(tok_rows, top_count)
    places = jnp.arange(n_experts * capacity, dtype=jnp.int32)
    placing = jnp.sum((places[:, None, None] == target[None, :, :]).astype(jnp.int32), -1).astype(
        jnp.bfloat16
    )
    sent = jnp.dot(placing, normed, preferred_element_type=jnp.float32).astype(jnp.bfloat16)
    sent = sent.reshape(n_experts, capacity, normed.shape[1])
    block = lax.all_to_all(sent, ("attn", "exp"), split_axis=0, concat_axis=0, tiled=True)
    n_src = block.shape[0] // exp_dev
    rows_four = block.reshape(n_src, exp_dev, block.shape[1], block.shape[2])
    both = jnp.einsum("sjmd,jdf->sjmf", rows_four, w_gate_up, preferred_element_type=jnp.float32)
    hidden = (jax.nn.silu(both[..., :hidden_units]) * both[..., hidden_units:]).astype(jnp.bfloat16)
    result = jnp.einsum("sjmf,jfd->sjmd", hidden, w_down, preferred_element_type=jnp.float32)
    result = result.astype(jnp.bfloat16).reshape(block.shape)
    returned = lax.all_to_all(result, ("attn", "exp"), split_axis=0, concat_axis=0, tiled=True)
    picked = (
        returned[flat_ids, slot].reshape(tok_rows, top_count, normed.shape[1]).astype(jnp.float32)
    )
    numer = gate_nums.astype(jnp.float32)
    weights = numer / jnp.sum(numer, -1, keepdims=True)
    return middle + jnp.sum(picked * weights[:, :, None], 1)


def fits_grid(mesh):
    return mesh.shape["attn"] == 4 and mesh.shape["exp"] == 4


def solution(mesh):
    in_specs = (
        P(("groups", "exp"), None, "attn"),
        P(("groups", "exp"), None, "attn"),
        P(("groups", "exp"), None, "attn"),
        P(("groups", "exp"), None, "attn"),
        P(("groups", "exp"), None, "attn"),
        P(("groups", "exp")),
        P("attn", "exp"),
        P(("groups", "exp", "attn"), None),
        P(),
        P(("groups", "exp", "attn"), None),
        P(("groups", "exp", "attn"), None),
        P(("attn", "exp"), None, None),
        P(("attn", "exp"), None, None),
    )
    out_specs = P(("groups", "exp", "attn"), None)
    body = grid_shards if fits_grid(mesh) else shards
    return jax.shard_map(body, mesh=mesh, in_specs=in_specs, out_specs=out_specs, check_vma=False)
```

```python
import jax
import jax.numpy as jnp
from jax import lax
from jax.experimental import pallas as pl
from jax.experimental.pallas import tpu as pltpu
from jax.sharding import PartitionSpec as P

HD = 128
LANES = 128
F32 = jnp.float32
BF16 = jnp.bfloat16


def places():
    a = lax.axis_index("attn")
    z = lax.axis_index("exp")
    core = a + 1 - 2 * (a % 2)
    across = (a + 2) % 4
    planes = [z, z + 1 - 2 * (z % 2), (z + 2) % 4, 3 - z]
    return a, z, core, across, planes


def meet(a, z, core, across, planes):
    barrier = pltpu.get_barrier_semaphore()
    peers = [(core, z), (across, z)] + [(a, p) for p in planes[1:]]
    for pa, pz in peers:
        pl.semaphore_signal(
            barrier,
            inc=1,
            device_id={"attn": pa, "exp": pz},
            device_id_type=pl.DeviceIdType.MESH,
        )
    pl.semaphore_wait(barrier, len(peers))


def copy_to(src, dst, sems, i, pa, pz):
    return pltpu.make_async_remote_copy(
        src_ref=src,
        dst_ref=dst,
        send_sem=sems[0].at[i],
        recv_sem=sems[1].at[i],
        device_id={"attn": pa, "exp": pz},
        device_id_type=pl.DeviceIdType.MESH,
    )


def attend(q, k_new, v_new, k_old, v_old, length):
    n_new, n_old = q.shape[0], k_old.shape[0]
    kv_count = k_old.shape[1] // HD
    group = q.shape[1] // (kv_count * HD)
    scale = 1.0 / HD**0.5
    dims = (((1,), (1,)), ((), ()))
    heads = []
    for j in range(kv_count):
        cols = slice(j * HD, (j + 1) * HD)
        rows = jnp.concatenate(
            [q[:, (j * group + g) * HD : (j * group + g + 1) * HD] for g in range(group)], 0
        )
        s_old = lax.dot_general(rows, k_old[:, cols], dims, preferred_element_type=F32) * scale
        s_new = lax.dot_general(rows, k_new[:, cols], dims, preferred_element_type=F32) * scale
        valid = lax.broadcasted_iota(jnp.int32, s_old.shape, 1) < length
        s_old = jnp.where(valid, s_old, F32(-1e30))
        token = lax.broadcasted_iota(jnp.int32, (group, n_new, n_new), 1).reshape(s_new.shape)
        causal = lax.broadcasted_iota(jnp.int32, s_new.shape, 1) <= token
        s_new = jnp.where(causal, s_new, F32(-1e30))
        top = jnp.maximum(jnp.max(s_old, -1, keepdims=True), jnp.max(s_new, -1, keepdims=True))
        e_old = jnp.exp(s_old - top)
        e_new = jnp.exp(s_new - top)
        inv = 1.0 / (jnp.sum(e_old, -1, keepdims=True) + jnp.sum(e_new, -1, keepdims=True))
        p_old = (e_old * inv).astype(BF16)
        p_new = (e_new * inv).astype(BF16)
        out = jnp.dot(p_old, v_old[:, cols], preferred_element_type=F32)
        out = out + jnp.dot(p_new, v_new[:, cols], preferred_element_type=F32)
        out = out.astype(BF16)
        heads += [out[g * n_new : (g + 1) * n_new] for g in range(group)]
    return jnp.concatenate(heads, 1)


def layer_kernel(
    len_ref, q_hbm, kn_hbm, vn_hbm, kc_hbm, vc_hbm, wo_hbm, res_hbm, wgu_hbm, wd_hbm,
    gain_ref, ids_ref, gates_ref, mixed_ref, *scratch,
):
    n_project = 19
    a, z, core, across, planes = places()
    wgu, wd, xall, middle, wsem = scratch[n_project : n_project + 5]
    loads = [
        pltpu.make_async_copy(wgu_hbm.at[0], wgu, wsem.at[0]),
        pltpu.make_async_copy(wd_hbm.at[0], wd, wsem.at[1]),
        pltpu.make_async_copy(res_hbm, middle, wsem.at[2]),
    ]
    project_part(
        len_ref, q_hbm, kn_hbm, vn_hbm, kc_hbm, vc_hbm, wo_hbm, mixed_ref, loads,
        *scratch[:n_project],
    )
    loads[2].wait()
    width = mixed_ref.shape[1]
    middle[...] += mixed_ref[...]
    m = middle[...]
    meansq = jnp.mean(m * m, -1, keepdims=True)
    xall[0, 0, :, :width] = (m * lax.rsqrt(meansq + 1e-06) * gain_ref[...]).astype(BF16)
    expert = lax.broadcasted_iota(jnp.int32, (LANES, m.shape[0]), 0)
    nums = jnp.zeros((LANES, m.shape[0]), F32)
    for k in range(ids_ref.shape[0]):
        num = gates_ref[k : k + 1, :].astype(F32)
        nums = nums + jnp.where(expert == ids_ref[k : k + 1, :], num, F32(0))
    xall[0, 0, :, width:] = nums.T.astype(BF16)
    experts_part(mixed_ref, loads, *scratch[n_project:])


def project_part(
    len_ref, q_hbm, kn_hbm, vn_hbm, kc_hbm, vc_hbm, wo_hbm, out_ref, later,
    q_ref, kn_ref, vn_ref, kc_ref, vc_ref, wo_ref, lsem, att, own, csend, crecv, xsend, xrecv, zsend, zrecv, gs, gr, ss, sr,
):
    a, z, core, across, planes = places()
    opposite = (core + 2) % 4
    loads = [
        pltpu.make_async_copy(src, dst, lsem.at[i])
        for i, (src, dst) in enumerate(
            [
                (q_hbm, q_ref),
                (kn_hbm, kn_ref),
                (vn_hbm, vn_ref),
                (kc_hbm, kc_ref),
                (vc_hbm, vc_ref),
                (wo_hbm, wo_ref),
            ]
        )
    ]
    for load in loads + later:
        load.start()
    meet(a, z, core, across, planes)
    for load in loads:
        load.wait()
    g, s = (gs, gr), (ss, sr)
    n_chunk, rows = att.shape[1], att.shape[2]
    n_new = q_ref.shape[1]
    per = rows // n_new
    width = wo_ref.shape[1]

    def chunk_copy(k, j):
        src = att.at[2, j] if k == 3 else att.at[0, j]
        return copy_to(src, att.at[k, j], g, (k - 1) * n_chunk + j, a, planes[2 if k == 2 else 1])

    @pl.loop(0, n_chunk)
    def _(j):
        for i in range(per):
            t = j * per + i
            att[0, j, i * n_new : (i + 1) * n_new, :] = attend(
                q_ref[t], kn_ref[t], vn_ref[t], kc_ref[t], vc_ref[t], len_ref[t]
            )
        chunk_copy(2, j).start()
        chunk_copy(1, j).start()

    def product(k):
        x = jnp.concatenate([att[k, a], att[k, across], att[k, core], att[k, opposite]], 0)
        r = jnp.dot(x, wo_ref[...], preferred_element_type=F32)
        own[k] = r[: 2 * rows]
        csend[k] = r[2 * rows :]
        core_copy(k).start()

    def core_copy(k):
        return copy_to(csend.at[k], crecv.at[k], s, k, core, z)

    def x_copy(k):
        return copy_to(xsend.at[k], xrecv.at[k], s, 4 + k, across, z)

    def z_copy(k):
        return copy_to(zsend.at[k - 1], zrecv.at[k - 1], s, 7 + k, a, planes[k])

    def to_x(k):
        core_copy(k).wait_recv()
        xsend[k] = (own[k, rows:, :] + crecv[k, rows:, :]).astype(BF16)
        x_copy(k).start()

    def to_z(k):
        x_copy(k).wait_recv()
        total = own[k, :rows, :] + crecv[k, :rows, :] + xrecv[k].astype(F32)
        if k == 0:
            out_ref[:, pl.ds(pl.multiple_of(z * width, LANES), width)] = total
        else:
            zsend[k - 1] = total.astype(BF16)
            z_copy(k).start()

    @pl.loop(0, n_chunk)
    def _(j):
        chunk_copy(2, j).wait_recv()
        chunk_copy(3, j).start()

    product(0)
    for j in range(n_chunk):
        chunk_copy(1, j).wait_recv()
    product(1)
    to_x(0)
    product(2)
    to_x(1)
    to_z(0)
    to_x(2)
    to_z(1)
    to_z(2)
    for j in range(n_chunk):
        chunk_copy(3, j).wait_recv()
    product(3)
    to_x(3)
    to_z(3)
    for k in range(1, 4):
        z_copy(k).wait_recv()
        out_ref[:, pl.ds(pl.multiple_of(planes[k] * width, LANES), width)] = zrecv[k - 1].astype(F32)

    @pl.loop(0, n_chunk)
    def _(j):
        for k in range(1, 4):
            chunk_copy(k, j).wait_send()

    for k in range(4):
        core_copy(k).wait_send()
        x_copy(k).wait_send()
        if k > 0:
            z_copy(k).wait_send()


def experts_part(
    out_ref, loads,
    wgu, wd, xall, middle, wsem, hid, own, csend, crecv, xsend, xrecv, zsend, zrecv, gs, gr, ss, sr,
):
    a, z, core, across, planes = places()
    load_gu, load_d = loads[:2]
    g, s = (gs, gr), (ss, sr)
    rows, width = out_ref.shape
    units = wd.shape[0]
    mine = a * 4 + z

    half = rows // 2

    def part(ref, h):
        return ref.at[pl.ds(h * half, half), :]

    def rows_copy(ks, i, kd, j, index, h, pa, pz):
        return copy_to(
            part(xall.at[ks, i], h), part(xall.at[kd, j], h), g, 2 * index + h, pa, pz
        )

    def z_in(k, h):
        return rows_copy(2 if k == 3 else 0, 0, k, 0, k - 1, h, a, planes[2 if k == 2 else 1])

    def x_in(k, h):
        if k == 1:
            return rows_copy(0, 1, 1, 1, 4, h, a, planes[1])
        return rows_copy(k, 0, k, 1, 3 + k, h, across, z)

    def core_in(k, i, h):
        return rows_copy(k, i, k, 2 + i, 7 + 2 * k + i, h, core, z)

    def core_copy(k, h):
        return copy_to(csend.at[k, h], crecv.at[k, h], s, 2 * k + h, core, z)

    def x_copy(k, h):
        return copy_to(xsend.at[k, h], xrecv.at[k, h], s, 2 * (4 + k) + h, across, z)

    def z_copy(k, h):
        return copy_to(zsend.at[k - 1, h], zrecv.at[k - 1, h], s, 2 * (7 + k) + h, a, planes[k])

    def compute(k):
        for i in range(2):
            for h in range(2):
                core_in(k, i, h).wait_recv()
        if k == 0:
            load_gu.wait()
        x = xall[k].reshape(4 * rows, width + LANES)[:, :width]
        nums = xall[k].reshape(4 * rows, width + LANES)[:, width:].astype(F32)
        lane = lax.broadcasted_iota(jnp.int32, nums.shape, 1)
        num = jnp.sum(jnp.where(lane == mine, nums, F32(0)), -1, keepdims=True)
        weight = num / jnp.sum(nums, -1, keepdims=True)

        @pl.loop(0, units // 256)
        def _(t):
            at = pl.multiple_of(t * 256, 256)
            gate = jnp.dot(x, wgu[:, pl.ds(at, 256)], preferred_element_type=F32)
            up = jnp.dot(
                x,
                wgu[:, pl.ds(pl.multiple_of(units + t * 256, 256), 256)],
                preferred_element_type=F32,
            )
            hid[:, pl.ds(at, 256)] = (gate / (1.0 + jnp.exp(-gate)) * up).astype(BF16)

        if k == 0:
            load_d.wait()

        for h in range(2):
            for t in range(2):
                lo = h * (width // 2) + t * (width // 4)
                r = jnp.dot(hid[...], wd[:, lo : lo + width // 4], preferred_element_type=F32)
                r = r * weight
                at = slice(t * (width // 4), (t + 1) * (width // 4))
                own[k, h, :, at] = r[: 2 * rows]
                csend[k, h, :, at] = r[2 * rows :].astype(BF16)
            core_copy(k, h).start()

    def to_x(k):
        for h in range(2):
            core_copy(k, h).wait_recv()
            total = own[k, h, rows:, :] + crecv[k, h, rows:, :].astype(F32)
            xsend[k, h] = total.astype(BF16)
            x_copy(k, h).start()

    def to_z(k):
        for h in range(2):
            x_copy(k, h).wait_recv()
            total = own[k, h, :rows, :] + crecv[k, h, :rows, :].astype(F32)
            total = total + xrecv[k, h].astype(F32)
            if k == 0:
                at = slice(h * (width // 2), (h + 1) * (width // 2))
                out_ref[:, at] = middle[:, at] + total
            else:
                zsend[k - 1, h] = total.astype(BF16)
                z_copy(k, h).start()

    for h in range(2):
        z_in(2, h).start()
        x_in(0, h).start()
        core_in(0, 0, h).start()
    for h in range(2):
        z_in(1, h).start()

    def pass_z(k):
        for h in range(2):
            z_in(k, h).wait_recv()
            if k == 2:
                z_in(3, h).start()
            if k != 1:
                x_in(k, h).start()
            core_in(k, 0, h).start()

    def pass_x(k):
        for h in range(2):
            x_in(k, h).wait_recv()
            if k == 0:
                x_in(1, h).start()
            core_in(k, 1, h).start()

    pass_x(0)
    pass_z(2)
    pass_z(1)
    compute(0)
    pass_z(3)
    pass_x(1)
    compute(1)
    pass_x(2)
    to_x(1)
    pass_x(3)
    compute(2)
    to_x(2)
    to_z(1)
    compute(3)
    to_x(3)
    to_x(0)
    to_z(2)
    to_z(3)
    to_z(0)
    for h in range(2):
        at = slice(h * (width // 2), (h + 1) * (width // 2))
        for k in range(1, 4):
            z_copy(k, h).wait_recv()
            out_ref[:, at] += zrecv[k - 1, h].astype(F32)
    for k in range(4):
        for h in range(2):
            x_in(k, h).wait_send()
            core_in(k, 0, h).wait_send()
            core_in(k, 1, h).wait_send()
            core_copy(k, h).wait_send()
            x_copy(k, h).wait_send()
            if k > 0:
                z_in(k, h).wait_send()
                z_copy(k, h).wait_send()


def grid_shards(
    queries,
    new_keys,
    new_values,
    cache_keys,
    cache_values,
    cache_len,
    out_weight,
    residual,
    norm_gain,
    expert_ids,
    gate_nums,
    w_gate_up,
    w_down,
):
    rows, width = residual.shape
    units = w_down.shape[1]
    cols = out_weight.shape[1]
    heads = queries.shape[2]
    vmem = pl.BlockSpec(memory_space=pltpu.VMEM)
    hbm = pl.BlockSpec(memory_space=pl.ANY)
    return pl.pallas_call(
        layer_kernel,
        out_shape=jax.ShapeDtypeStruct((rows, width), F32),
        in_specs=[pl.BlockSpec(memory_space=pltpu.SMEM)] + [hbm] * 9 + [vmem] * 3,
        out_specs=vmem,
        scratch_shapes=[
            pltpu.VMEM(queries.shape, BF16),
            pltpu.VMEM(new_keys.shape, BF16),
            pltpu.VMEM(new_values.shape, BF16),
            pltpu.VMEM(cache_keys.shape, BF16),
            pltpu.VMEM(cache_values.shape, BF16),
            pltpu.VMEM(out_weight.shape, BF16),
            pltpu.SemaphoreType.DMA((6,)),
            pltpu.VMEM((4, 4, rows, heads), BF16),
            pltpu.VMEM((4, 2 * rows, cols), F32),
            pltpu.VMEM((4, 2 * rows, cols), F32),
            pltpu.VMEM((4, 2 * rows, cols), F32),
            pltpu.VMEM((4, rows, cols), BF16),
            pltpu.VMEM((4, rows, cols), BF16),
            pltpu.VMEM((3, rows, cols), BF16),
            pltpu.VMEM((3, rows, cols), BF16),
            pltpu.SemaphoreType.DMA((12,)),
            pltpu.SemaphoreType.DMA((12,)),
            pltpu.SemaphoreType.DMA((11,)),
            pltpu.SemaphoreType.DMA((11,)),
            pltpu.VMEM((width, 2 * units), BF16),
            pltpu.VMEM((units, width), BF16),
            pltpu.VMEM((4, 4, rows, width + LANES), BF16),
            pltpu.VMEM((rows, width), F32),
            pltpu.SemaphoreType.DMA((3,)),
            pltpu.VMEM((4 * rows, units), BF16),
            pltpu.VMEM((4, 2, 2 * rows, width // 2), F32),
            pltpu.VMEM((4, 2, 2 * rows, width // 2), BF16),
            pltpu.VMEM((4, 2, 2 * rows, width // 2), BF16),
            pltpu.VMEM((4, 2, rows, width // 2), BF16),
            pltpu.VMEM((4, 2, rows, width // 2), BF16),
            pltpu.VMEM((3, 2, rows, width // 2), BF16),
            pltpu.VMEM((3, 2, rows, width // 2), BF16),
            pltpu.SemaphoreType.DMA((30,)),
            pltpu.SemaphoreType.DMA((30,)),
            pltpu.SemaphoreType.DMA((22,)),
            pltpu.SemaphoreType.DMA((22,)),
        ],
        compiler_params=pltpu.CompilerParams(
            collective_id=0, has_side_effects=True, vmem_limit_bytes=58 << 20
        ),
    )(
        cache_len, queries, new_keys, new_values, cache_keys, cache_values, out_weight,
        residual, w_gate_up, w_down, norm_gain.reshape(1, width), expert_ids.T, gate_nums.T,
    )


def attend_session(packed):
    q_s, k_new, v_new, k_old, v_old, length = packed
    n_new = q_s.shape[0]
    n_old = k_old.shape[0]
    kv_count = k_old.shape[-1] // HD
    group_size = q_s.shape[-1] // (kv_count * HD)
    q_four = q_s.reshape(n_new, kv_count, group_size, HD)
    k_old3 = k_old.reshape(n_old, kv_count, HD)
    v_old3 = v_old.reshape(n_old, kv_count, HD)
    k_new3 = k_new.reshape(n_new, kv_count, HD)
    v_new3 = v_new.reshape(n_new, kv_count, HD)
    scale = 1.0 / HD**0.5
    s_old = jnp.einsum("ikgd,jkd->kgij", q_four, k_old3, preferred_element_type=jnp.float32) * scale
    s_new = jnp.einsum("ikgd,jkd->kgij", q_four, k_new3, preferred_element_type=jnp.float32) * scale
    valid_old = jnp.arange(n_old, dtype=jnp.int32) < length
    s_old = jnp.where(valid_old[None, None, None, :], s_old, jnp.float32(-1e30))
    causal = (
        jnp.arange(n_new, dtype=jnp.int32)[None, :] <= jnp.arange(n_new, dtype=jnp.int32)[:, None]
    )
    s_new = jnp.where(causal[None, None], s_new, jnp.float32(-1e30))
    top = jnp.maximum(jnp.max(s_old, -1, keepdims=True), jnp.max(s_new, -1, keepdims=True))
    e_old = jnp.exp(s_old - top)
    e_new = jnp.exp(s_new - top)
    total = jnp.sum(e_old, -1, keepdims=True) + jnp.sum(e_new, -1, keepdims=True)
    p_old = (e_old / total).astype(jnp.bfloat16)
    p_new = (e_new / total).astype(jnp.bfloat16)
    out = jnp.einsum("kgij,jkd->ikgd", p_old, v_old3, preferred_element_type=jnp.float32)
    out = out + jnp.einsum("kgij,jkd->ikgd", p_new, v_new3, preferred_element_type=jnp.float32)
    return out.reshape(n_new, kv_count * group_size * HD).astype(jnp.bfloat16)


def shards(
    queries,
    new_keys,
    new_values,
    cache_keys,
    cache_values,
    cache_len,
    out_weight,
    residual,
    norm_gain,
    expert_ids,
    gate_nums,
    w_gate_up,
    w_down,
):
    attended = lax.map(
        attend_session, (queries, new_keys, new_values, cache_keys, cache_values, cache_len)
    )
    local_rows = attended.reshape(attended.shape[0] * attended.shape[1], attended.shape[2])
    spread = jnp.dot(
        lax.all_gather(local_rows, "exp", axis=0, tiled=True),
        out_weight,
        preferred_element_type=jnp.float32,
    )
    partial_value = lax.all_to_all(spread, "exp", split_axis=0, concat_axis=1, tiled=True)
    projected = lax.psum_scatter(partial_value, "attn", scatter_dimension=0, tiled=True)
    middle = residual + projected
    meansq = jnp.mean(middle * middle, -1, keepdims=True)
    normed = (middle * lax.rsqrt(meansq + 1e-06) * norm_gain).astype(jnp.bfloat16)
    tok_rows = expert_ids.shape[0]
    top_count = expert_ids.shape[1]
    exp_dev = w_gate_up.shape[0]
    hidden_units = w_down.shape[1]
    n_experts = exp_dev * lax.axis_size("attn") * lax.axis_size("exp")
    capacity = max(2, 2 * tok_rows * top_count // n_experts)
    flat_ids = expert_ids.reshape(-1)
    onehot = (flat_ids[:, None] == jnp.arange(n_experts, dtype=jnp.int32)[None, :]).astype(
        jnp.int32
    )
    before = jnp.cumsum(onehot, axis=0) - onehot
    slot = jnp.sum(before * onehot, -1)
    target = (flat_ids * capacity + slot).reshape(tok_rows, top_count)
    places = jnp.arange(n_experts * capacity, dtype=jnp.int32)
    placing = jnp.sum((places[:, None, None] == target[None, :, :]).astype(jnp.int32), -1).astype(
        jnp.bfloat16
    )
    sent = jnp.dot(placing, normed, preferred_element_type=jnp.float32).astype(jnp.bfloat16)
    sent = sent.reshape(n_experts, capacity, normed.shape[1])
    block = lax.all_to_all(sent, ("attn", "exp"), split_axis=0, concat_axis=0, tiled=True)
    n_src = block.shape[0] // exp_dev
    rows_four = block.reshape(n_src, exp_dev, block.shape[1], block.shape[2])
    both = jnp.einsum("sjmd,jdf->sjmf", rows_four, w_gate_up, preferred_element_type=jnp.float32)
    hidden = (jax.nn.silu(both[..., :hidden_units]) * both[..., hidden_units:]).astype(jnp.bfloat16)
    result = jnp.einsum("sjmf,jfd->sjmd", hidden, w_down, preferred_element_type=jnp.float32)
    result = result.astype(jnp.bfloat16).reshape(block.shape)
    returned = lax.all_to_all(result, ("attn", "exp"), split_axis=0, concat_axis=0, tiled=True)
    picked = (
        returned[flat_ids, slot].reshape(tok_rows, top_count, normed.shape[1]).astype(jnp.float32)
    )
    numer = gate_nums.astype(jnp.float32)
    weights = numer / jnp.sum(numer, -1, keepdims=True)
    return middle + jnp.sum(picked * weights[:, :, None], 1)


def fits_grid(mesh):
    return mesh.shape["attn"] == 4 and mesh.shape["exp"] == 4


def solution(mesh):
    in_specs = (
        P(("groups", "exp"), None, "attn"),
        P(("groups", "exp"), None, "attn"),
        P(("groups", "exp"), None, "attn"),
        P(("groups", "exp"), None, "attn"),
        P(("groups", "exp"), None, "attn"),
        P(("groups", "exp")),
        P("attn", "exp"),
        P(("groups", "exp", "attn"), None),
        P(),
        P(("groups", "exp", "attn"), None),
        P(("groups", "exp", "attn"), None),
        P(("attn", "exp"), None, None),
        P(("attn", "exp"), None, None),
    )
    out_specs = P(("groups", "exp", "attn"), None)
    body = grid_shards if fits_grid(mesh) else shards
    return jax.shard_map(body, mesh=mesh, in_specs=in_specs, out_specs=out_specs, check_vma=False)
```

```python
import jax
import jax.numpy as jnp
from jax import lax
from jax.experimental import pallas as pl
from jax.experimental.pallas import tpu as pltpu
from jax.sharding import PartitionSpec as P

HD = 128
LANES = 128
F32 = jnp.float32
BF16 = jnp.bfloat16


def places():
    a = lax.axis_index("attn")
    z = lax.axis_index("exp")
    core = a + 1 - 2 * (a % 2)
    across = (a + 2) % 4
    planes = [z, z + 1 - 2 * (z % 2), (z + 2) % 4, 3 - z]
    return a, z, core, across, planes


def meet(a, z, core, across, planes):
    barrier = pltpu.get_barrier_semaphore()
    peers = [(core, z), (across, z)] + [(a, p) for p in planes[1:]]
    for pa, pz in peers:
        pl.semaphore_signal(
            barrier,
            inc=1,
            device_id={"attn": pa, "exp": pz},
            device_id_type=pl.DeviceIdType.MESH,
        )
    pl.semaphore_wait(barrier, len(peers))


def copy_to(src, dst, sems, i, pa, pz):
    return pltpu.make_async_remote_copy(
        src_ref=src,
        dst_ref=dst,
        send_sem=sems[0].at[i],
        recv_sem=sems[1].at[i],
        device_id={"attn": pa, "exp": pz},
        device_id_type=pl.DeviceIdType.MESH,
    )


def attend(q, k_new, v_new, k_old, v_old, length):
    n_new, n_old = q.shape[0], k_old.shape[0]
    kv_count = k_old.shape[1] // HD
    group = q.shape[1] // (kv_count * HD)
    scale = 1.0 / HD**0.5
    dims = (((1,), (1,)), ((), ()))
    heads = []
    for j in range(kv_count):
        cols = slice(j * HD, (j + 1) * HD)
        rows = jnp.concatenate(
            [q[:, (j * group + g) * HD : (j * group + g + 1) * HD] for g in range(group)], 0
        )
        s_old = lax.dot_general(rows, k_old[:, cols], dims, preferred_element_type=F32) * scale
        s_new = lax.dot_general(rows, k_new[:, cols], dims, preferred_element_type=F32) * scale
        valid = lax.broadcasted_iota(jnp.int32, s_old.shape, 1) < length
        s_old = jnp.where(valid, s_old, F32(-1e30))
        token = lax.broadcasted_iota(jnp.int32, (group, n_new, n_new), 1).reshape(s_new.shape)
        causal = lax.broadcasted_iota(jnp.int32, s_new.shape, 1) <= token
        s_new = jnp.where(causal, s_new, F32(-1e30))
        top = jnp.maximum(jnp.max(s_old, -1, keepdims=True), jnp.max(s_new, -1, keepdims=True))
        e_old = jnp.exp(s_old - top)
        e_new = jnp.exp(s_new - top)
        inv = 1.0 / (jnp.sum(e_old, -1, keepdims=True) + jnp.sum(e_new, -1, keepdims=True))
        p_old = (e_old * inv).astype(BF16)
        p_new = (e_new * inv).astype(BF16)
        out = jnp.dot(p_old, v_old[:, cols], preferred_element_type=F32)
        out = out + jnp.dot(p_new, v_new[:, cols], preferred_element_type=F32)
        out = out.astype(BF16)
        heads += [out[g * n_new : (g + 1) * n_new] for g in range(group)]
    return jnp.concatenate(heads, 1)


def layer_kernel(
    len_ref, q_hbm, kn_hbm, vn_hbm, kc_hbm, vc_hbm, wo_hbm, res_hbm, wgu_hbm, wd_hbm,
    gain_ref, ids_ref, gates_ref, mixed_ref, *scratch,
):
    n_project = 19
    a, z, core, across, planes = places()
    wgu, wd, xall, middle, wsem = scratch[n_project : n_project + 5]
    loads = [
        pltpu.make_async_copy(wgu_hbm.at[0], wgu, wsem.at[0]),
        pltpu.make_async_copy(wd_hbm.at[0], wd, wsem.at[1]),
        pltpu.make_async_copy(res_hbm, middle, wsem.at[2]),
    ]
    project_part(
        len_ref, q_hbm, kn_hbm, vn_hbm, kc_hbm, vc_hbm, wo_hbm, mixed_ref, loads,
        *scratch[:n_project],
    )
    loads[2].wait()
    width = mixed_ref.shape[1]
    middle[...] += mixed_ref[...]
    m = middle[...]
    meansq = jnp.mean(m * m, -1, keepdims=True)
    xall[0, 0, :, :width] = (m * lax.rsqrt(meansq + 1e-06) * gain_ref[...]).astype(BF16)
    expert = lax.broadcasted_iota(jnp.int32, (LANES, m.shape[0]), 0)
    nums = jnp.zeros((LANES, m.shape[0]), F32)
    for k in range(ids_ref.shape[0]):
        num = gates_ref[k : k + 1, :].astype(F32)
        nums = nums + jnp.where(expert == ids_ref[k : k + 1, :], num, F32(0))
    xall[0, 0, :, width:] = nums.T.astype(BF16)
    experts_part(mixed_ref, loads, *scratch[n_project:])


def project_part(
    len_ref, q_hbm, kn_hbm, vn_hbm, kc_hbm, vc_hbm, wo_hbm, out_ref, later,
    q_ref, kn_ref, vn_ref, kc_ref, vc_ref, wo_ref, lsem, att, own, csend, crecv, xsend, xrecv, zsend, zrecv, gs, gr, ss, sr,
):
    a, z, core, across, planes = places()
    opposite = (core + 2) % 4
    loads = [
        pltpu.make_async_copy(src, dst, lsem.at[i])
        for i, (src, dst) in enumerate(
            [
                (q_hbm, q_ref),
                (kn_hbm, kn_ref),
                (vn_hbm, vn_ref),
                (kc_hbm, kc_ref),
                (vc_hbm, vc_ref),
                (wo_hbm, wo_ref),
            ]
        )
    ]
    for load in loads + later:
        load.start()
    meet(a, z, core, across, planes)
    for load in loads:
        load.wait()
    g, s = (gs, gr), (ss, sr)
    n_chunk, rows = att.shape[1], att.shape[2]
    n_new = q_ref.shape[1]
    per = rows // n_new
    width = wo_ref.shape[1]

    def chunk_copy(k, j):
        src = att.at[2, j] if k == 3 else att.at[0, j]
        return copy_to(src, att.at[k, j], g, (k - 1) * n_chunk + j, a, planes[2 if k == 2 else 1])

    @pl.loop(0, n_chunk)
    def _(j):
        for i in range(per):
            t = j * per + i
            att[0, j, i * n_new : (i + 1) * n_new, :] = attend(
                q_ref[t], kn_ref[t], vn_ref[t], kc_ref[t], vc_ref[t], len_ref[t]
            )
        chunk_copy(2, j).start()
        chunk_copy(1, j).start()

    def product(k):
        x = jnp.concatenate([att[k, a], att[k, across], att[k, core], att[k, opposite]], 0)
        r = jnp.dot(x, wo_ref[...], preferred_element_type=F32)
        own[k] = r[: 2 * rows]
        csend[k] = r[2 * rows :]
        core_copy(k).start()

    def core_copy(k):
        return copy_to(csend.at[k], crecv.at[k], s, k, core, z)

    def x_copy(k):
        return copy_to(xsend.at[k], xrecv.at[k], s, 4 + k, across, z)

    def z_copy(k):
        return copy_to(zsend.at[k - 1], zrecv.at[k - 1], s, 7 + k, a, planes[k])

    def to_x(k):
        core_copy(k).wait_recv()
        xsend[k] = (own[k, rows:, :] + crecv[k, rows:, :]).astype(BF16)
        x_copy(k).start()

    def to_z(k):
        x_copy(k).wait_recv()
        total = own[k, :rows, :] + crecv[k, :rows, :] + xrecv[k].astype(F32)
        if k == 0:
            out_ref[:, pl.ds(pl.multiple_of(z * width, LANES), width)] = total
        else:
            zsend[k - 1] = total.astype(BF16)
            z_copy(k).start()

    @pl.loop(0, n_chunk)
    def _(j):
        chunk_copy(2, j).wait_recv()
        chunk_copy(3, j).start()

    product(0)
    for j in range(n_chunk):
        chunk_copy(1, j).wait_recv()
    product(1)
    to_x(0)
    product(2)
    to_x(1)
    to_z(0)
    to_x(2)
    to_z(1)
    to_z(2)
    for j in range(n_chunk):
        chunk_copy(3, j).wait_recv()
    product(3)
    to_x(3)
    to_z(3)
    for k in range(1, 4):
        z_copy(k).wait_recv()
        out_ref[:, pl.ds(pl.multiple_of(planes[k] * width, LANES), width)] = zrecv[k - 1].astype(F32)

    @pl.loop(0, n_chunk)
    def _(j):
        for k in range(1, 4):
            chunk_copy(k, j).wait_send()

    for k in range(4):
        core_copy(k).wait_send()
        x_copy(k).wait_send()
        if k > 0:
            z_copy(k).wait_send()


def experts_part(
    out_ref, loads,
    wgu, wd, xall, middle, wsem, hid, own, csend, crecv, xsend, xrecv, zsend, zrecv, gs, gr, ss, sr,
):
    a, z, core, across, planes = places()
    load_gu, load_d = loads[:2]
    g, s = (gs, gr), (ss, sr)
    rows, width = out_ref.shape
    units = wd.shape[0]
    mine = a * 4 + z

    half = rows // 2

    def part(ref, h):
        return ref.at[pl.ds(h * half, half), :]

    def rows_copy(ks, i, kd, j, index, h, pa, pz):
        return copy_to(
            part(xall.at[ks, i], h), part(xall.at[kd, j], h), g, 2 * index + h, pa, pz
        )

    def z_in(k, h):
        return rows_copy(2 if k == 3 else 0, 0, k, 0, k - 1, h, a, planes[2 if k == 2 else 1])

    def x_in(k, h):
        if k == 1:
            return rows_copy(0, 1, 1, 1, 4, h, a, planes[1])
        return rows_copy(k, 0, k, 1, 3 + k, h, across, z)

    def core_in(k, i, h):
        return rows_copy(k, i, k, 2 + i, 7 + 2 * k + i, h, core, z)

    def core_copy(k, h):
        return copy_to(csend.at[k, h], crecv.at[k, h], s, 2 * k + h, core, z)

    def x_copy(k, h):
        return copy_to(xsend.at[k, h], xrecv.at[k, h], s, 2 * (4 + k) + h, across, z)

    def z_copy(k, h):
        return copy_to(zsend.at[k - 1, h], zrecv.at[k - 1, h], s, 2 * (7 + k) + h, a, planes[k])

    def compute(k):
        for i in range(2):
            for h in range(2):
                core_in(k, i, h).wait_recv()
        if k == 0:
            load_gu.wait()
        x = xall[k].reshape(4 * rows, width + LANES)[:, :width]
        nums = xall[k].reshape(4 * rows, width + LANES)[:, width:].astype(F32)
        lane = lax.broadcasted_iota(jnp.int32, nums.shape, 1)
        num = jnp.sum(jnp.where(lane == mine, nums, F32(0)), -1, keepdims=True)
        weight = num / jnp.sum(nums, -1, keepdims=True)

        @pl.loop(0, units // 256)
        def _(t):
            at = pl.multiple_of(t * 256, 256)
            gate = jnp.dot(x, wgu[:, pl.ds(at, 256)], preferred_element_type=F32)
            up = jnp.dot(
                x,
                wgu[:, pl.ds(pl.multiple_of(units + t * 256, 256), 256)],
                preferred_element_type=F32,
            )
            hid[:, pl.ds(at, 256)] = (gate / (1.0 + jnp.exp(-gate)) * up).astype(BF16)

        if k == 0:
            load_d.wait()

        for h in range(2):
            for t in range(2):
                lo = h * (width // 2) + t * (width // 4)
                r = jnp.dot(hid[...], wd[:, lo : lo + width // 4], preferred_element_type=F32)
                r = r * weight
                at = slice(t * (width // 4), (t + 1) * (width // 4))
                own[k, h, :, at] = r[: 2 * rows]
                csend[k, h, :, at] = r[2 * rows :].astype(BF16)
            core_copy(k, h).start()

    def to_x(k):
        for h in range(2):
            core_copy(k, h).wait_recv()
            total = own[k, h, rows:, :] + crecv[k, h, rows:, :].astype(F32)
            xsend[k, h] = total.astype(BF16)
            x_copy(k, h).start()

    def to_z(k):
        for h in range(2):
            x_copy(k, h).wait_recv()
            total = own[k, h, :rows, :] + crecv[k, h, :rows, :].astype(F32)
            total = total + xrecv[k, h].astype(F32)
            if k == 0:
                at = slice(h * (width // 2), (h + 1) * (width // 2))
                out_ref[:, at] = middle[:, at] + total
            else:
                zsend[k - 1, h] = total.astype(BF16)
                z_copy(k, h).start()

    for h in range(2):
        z_in(2, h).start()
        x_in(0, h).start()
        core_in(0, 0, h).start()
    z_in(1, 0).start()

    def pass_z(k):
        for h in range(2):
            z_in(k, h).wait_recv()
            if k == 2:
                z_in(3, h).start()
            if k != 1:
                x_in(k, h).start()
            core_in(k, 0, h).start()

    def pass_x(k):
        for h in range(2):
            x_in(k, h).wait_recv()
            core_in(k, 1, h).start()

    pass_x(0)
    pass_z(2)
    z_in(1, 1).start()
    for h in range(2):
        x_in(1, h).start()
    compute(0)
    pass_x(2)
    pass_z(3)
    compute(2)
    to_x(2)
    pass_x(3)
    pass_z(1)
    compute(3)
    to_x(3)
    to_z(2)
    pass_x(1)
    compute(1)
    to_x(1)
    to_x(0)
    to_z(3)
    to_z(1)
    to_z(0)
    for h in range(2):
        at = slice(h * (width // 2), (h + 1) * (width // 2))
        for k in range(1, 4):
            z_copy(k, h).wait_recv()
            out_ref[:, at] += zrecv[k - 1, h].astype(F32)
    for k in range(4):
        for h in range(2):
            x_in(k, h).wait_send()
            core_in(k, 0, h).wait_send()
            core_in(k, 1, h).wait_send()
            core_copy(k, h).wait_send()
            x_copy(k, h).wait_send()
            if k > 0:
                z_in(k, h).wait_send()
                z_copy(k, h).wait_send()


def grid_shards(
    queries,
    new_keys,
    new_values,
    cache_keys,
    cache_values,
    cache_len,
    out_weight,
    residual,
    norm_gain,
    expert_ids,
    gate_nums,
    w_gate_up,
    w_down,
):
    rows, width = residual.shape
    units = w_down.shape[1]
    cols = out_weight.shape[1]
    heads = queries.shape[2]
    vmem = pl.BlockSpec(memory_space=pltpu.VMEM)
    hbm = pl.BlockSpec(memory_space=pl.ANY)
    return pl.pallas_call(
        layer_kernel,
        out_shape=jax.ShapeDtypeStruct((rows, width), F32),
        in_specs=[pl.BlockSpec(memory_space=pltpu.SMEM)] + [hbm] * 9 + [vmem] * 3,
        out_specs=vmem,
        scratch_shapes=[
            pltpu.VMEM(queries.shape, BF16),
            pltpu.VMEM(new_keys.shape, BF16),
            pltpu.VMEM(new_values.shape, BF16),
            pltpu.VMEM(cache_keys.shape, BF16),
            pltpu.VMEM(cache_values.shape, BF16),
            pltpu.VMEM(out_weight.shape, BF16),
            pltpu.SemaphoreType.DMA((6,)),
            pltpu.VMEM((4, 4, rows, heads), BF16),
            pltpu.VMEM((4, 2 * rows, cols), F32),
            pltpu.VMEM((4, 2 * rows, cols), F32),
            pltpu.VMEM((4, 2 * rows, cols), F32),
            pltpu.VMEM((4, rows, cols), BF16),
            pltpu.VMEM((4, rows, cols), BF16),
            pltpu.VMEM((3, rows, cols), BF16),
            pltpu.VMEM((3, rows, cols), BF16),
            pltpu.SemaphoreType.DMA((12,)),
            pltpu.SemaphoreType.DMA((12,)),
            pltpu.SemaphoreType.DMA((11,)),
            pltpu.SemaphoreType.DMA((11,)),
            pltpu.VMEM((width, 2 * units), BF16),
            pltpu.VMEM((units, width), BF16),
            pltpu.VMEM((4, 4, rows, width + LANES), BF16),
            pltpu.VMEM((rows, width), F32),
            pltpu.SemaphoreType.DMA((3,)),
            pltpu.VMEM((4 * rows, units), BF16),
            pltpu.VMEM((4, 2, 2 * rows, width // 2), F32),
            pltpu.VMEM((4, 2, 2 * rows, width // 2), BF16),
            pltpu.VMEM((4, 2, 2 * rows, width // 2), BF16),
            pltpu.VMEM((4, 2, rows, width // 2), BF16),
            pltpu.VMEM((4, 2, rows, width // 2), BF16),
            pltpu.VMEM((3, 2, rows, width // 2), BF16),
            pltpu.VMEM((3, 2, rows, width // 2), BF16),
            pltpu.SemaphoreType.DMA((30,)),
            pltpu.SemaphoreType.DMA((30,)),
            pltpu.SemaphoreType.DMA((22,)),
            pltpu.SemaphoreType.DMA((22,)),
        ],
        compiler_params=pltpu.CompilerParams(
            collective_id=0, has_side_effects=True, vmem_limit_bytes=58 << 20
        ),
    )(
        cache_len, queries, new_keys, new_values, cache_keys, cache_values, out_weight,
        residual, w_gate_up, w_down, norm_gain.reshape(1, width), expert_ids.T, gate_nums.T,
    )


def attend_session(packed):
    q_s, k_new, v_new, k_old, v_old, length = packed
    n_new = q_s.shape[0]
    n_old = k_old.shape[0]
    kv_count = k_old.shape[-1] // HD
    group_size = q_s.shape[-1] // (kv_count * HD)
    q_four = q_s.reshape(n_new, kv_count, group_size, HD)
    k_old3 = k_old.reshape(n_old, kv_count, HD)
    v_old3 = v_old.reshape(n_old, kv_count, HD)
    k_new3 = k_new.reshape(n_new, kv_count, HD)
    v_new3 = v_new.reshape(n_new, kv_count, HD)
    scale = 1.0 / HD**0.5
    s_old = jnp.einsum("ikgd,jkd->kgij", q_four, k_old3, preferred_element_type=jnp.float32) * scale
    s_new = jnp.einsum("ikgd,jkd->kgij", q_four, k_new3, preferred_element_type=jnp.float32) * scale
    valid_old = jnp.arange(n_old, dtype=jnp.int32) < length
    s_old = jnp.where(valid_old[None, None, None, :], s_old, jnp.float32(-1e30))
    causal = (
        jnp.arange(n_new, dtype=jnp.int32)[None, :] <= jnp.arange(n_new, dtype=jnp.int32)[:, None]
    )
    s_new = jnp.where(causal[None, None], s_new, jnp.float32(-1e30))
    top = jnp.maximum(jnp.max(s_old, -1, keepdims=True), jnp.max(s_new, -1, keepdims=True))
    e_old = jnp.exp(s_old - top)
    e_new = jnp.exp(s_new - top)
    total = jnp.sum(e_old, -1, keepdims=True) + jnp.sum(e_new, -1, keepdims=True)
    p_old = (e_old / total).astype(jnp.bfloat16)
    p_new = (e_new / total).astype(jnp.bfloat16)
    out = jnp.einsum("kgij,jkd->ikgd", p_old, v_old3, preferred_element_type=jnp.float32)
    out = out + jnp.einsum("kgij,jkd->ikgd", p_new, v_new3, preferred_element_type=jnp.float32)
    return out.reshape(n_new, kv_count * group_size * HD).astype(jnp.bfloat16)


def shards(
    queries,
    new_keys,
    new_values,
    cache_keys,
    cache_values,
    cache_len,
    out_weight,
    residual,
    norm_gain,
    expert_ids,
    gate_nums,
    w_gate_up,
    w_down,
):
    attended = lax.map(
        attend_session, (queries, new_keys, new_values, cache_keys, cache_values, cache_len)
    )
    local_rows = attended.reshape(attended.shape[0] * attended.shape[1], attended.shape[2])
    spread = jnp.dot(
        lax.all_gather(local_rows, "exp", axis=0, tiled=True),
        out_weight,
        preferred_element_type=jnp.float32,
    )
    partial_value = lax.all_to_all(spread, "exp", split_axis=0, concat_axis=1, tiled=True)
    projected = lax.psum_scatter(partial_value, "attn", scatter_dimension=0, tiled=True)
    middle = residual + projected
    meansq = jnp.mean(middle * middle, -1, keepdims=True)
    normed = (middle * lax.rsqrt(meansq + 1e-06) * norm_gain).astype(jnp.bfloat16)
    tok_rows = expert_ids.shape[0]
    top_count = expert_ids.shape[1]
    exp_dev = w_gate_up.shape[0]
    hidden_units = w_down.shape[1]
    n_experts = exp_dev * lax.axis_size("attn") * lax.axis_size("exp")
    capacity = max(2, 2 * tok_rows * top_count // n_experts)
    flat_ids = expert_ids.reshape(-1)
    onehot = (flat_ids[:, None] == jnp.arange(n_experts, dtype=jnp.int32)[None, :]).astype(
        jnp.int32
    )
    before = jnp.cumsum(onehot, axis=0) - onehot
    slot = jnp.sum(before * onehot, -1)
    target = (flat_ids * capacity + slot).reshape(tok_rows, top_count)
    places = jnp.arange(n_experts * capacity, dtype=jnp.int32)
    placing = jnp.sum((places[:, None, None] == target[None, :, :]).astype(jnp.int32), -1).astype(
        jnp.bfloat16
    )
    sent = jnp.dot(placing, normed, preferred_element_type=jnp.float32).astype(jnp.bfloat16)
    sent = sent.reshape(n_experts, capacity, normed.shape[1])
    block = lax.all_to_all(sent, ("attn", "exp"), split_axis=0, concat_axis=0, tiled=True)
    n_src = block.shape[0] // exp_dev
    rows_four = block.reshape(n_src, exp_dev, block.shape[1], block.shape[2])
    both = jnp.einsum("sjmd,jdf->sjmf", rows_four, w_gate_up, preferred_element_type=jnp.float32)
    hidden = (jax.nn.silu(both[..., :hidden_units]) * both[..., hidden_units:]).astype(jnp.bfloat16)
    result = jnp.einsum("sjmf,jfd->sjmd", hidden, w_down, preferred_element_type=jnp.float32)
    result = result.astype(jnp.bfloat16).reshape(block.shape)
    returned = lax.all_to_all(result, ("attn", "exp"), split_axis=0, concat_axis=0, tiled=True)
    picked = (
        returned[flat_ids, slot].reshape(tok_rows, top_count, normed.shape[1]).astype(jnp.float32)
    )
    numer = gate_nums.astype(jnp.float32)
    weights = numer / jnp.sum(numer, -1, keepdims=True)
    return middle + jnp.sum(picked * weights[:, :, None], 1)


def fits_grid(mesh):
    return mesh.shape["attn"] == 4 and mesh.shape["exp"] == 4


def solution(mesh):
    in_specs = (
        P(("groups", "exp"), None, "attn"),
        P(("groups", "exp"), None, "attn"),
        P(("groups", "exp"), None, "attn"),
        P(("groups", "exp"), None, "attn"),
        P(("groups", "exp"), None, "attn"),
        P(("groups", "exp")),
        P("attn", "exp"),
        P(("groups", "exp", "attn"), None),
        P(),
        P(("groups", "exp", "attn"), None),
        P(("groups", "exp", "attn"), None),
        P(("attn", "exp"), None, None),
        P(("attn", "exp"), None, None),
    )
    out_specs = P(("groups", "exp", "attn"), None)
    body = grid_shards if fits_grid(mesh) else shards
    return jax.shard_map(body, mesh=mesh, in_specs=in_specs, out_specs=out_specs, check_vma=False)
```
